32 devices in a mesh: ty: 2 (over core), tx: 16 (over z, y, x).
Axes of the slice: x: 2, y: 2, z: 4, core: 2. Of those that a mesh axis runs over, the one named last changes fastest.
Arguments:
- movie: bfloat16 [64, 512, 128], P('ty', 'tx'), may hold values from 0 to 2
- footprints: bfloat16 [2, 16, 32, 1024], P('ty', 'tx'), may hold values from 0.049804688 to 1
- centres: int32 [2, 16, 32, 2], P('ty', 'tx'), may hold values from 0 to 31
- traces: bfloat16 [2, 16, 32, 128], P('ty', 'tx'), may hold values from 0 to 1
- counts: int32 [2, 16], P('ty', 'tx'), may hold values from 8 to 32
- order: int32 [2, 16, 32], P('ty', 'tx'), may hold values from 0 to 31, each once within a row
Outputs:
- new_traces: float32 [2, 16, 32, 128], P('ty', 'tx')
The draws below stay inside these ranges and needn't reach their ends.
Inputs may be any that keep to these rules, and one draw needn't show every extreme that they name: Slots 0 to counts - 1 of a tile hold neurons; the footprints, centres and traces of the other slots are not used. order[a, b] holds each of 0 to 31 once. `centres`: A centre lies inside its owner tile.
All inputs are finite; a program needn't handle non-finite values.
Results may differ from the reference program's by a relative error of at most 0.0003.
Values may be sent and summed in bfloat16 or wider, within the bound.
No kernel may reach another device: no remote copies, remote signals or barrier semaphores. Data moves between devices by JAX's collectives and lax.ppermute only.
A program may use at most 64 MiB of HBM per device.

```python
import jax
import jax.numpy as jnp
from jax import lax

TILE = 32
FRAMES = 128
K_DEV = 32
BLOCKS = 4
PATCH = 32
HEIGHT = 64
WIDTH = 512
N_TY = 2
N_TX = 16


def with_ends(drawn, stream_key, least, high):
    longest = drawn.shape.index(max(drawn.shape))
    spots = []
    for shift in (0, 1):
        where = [jax.random.randint(jax.random.fold_in(stream_key, axis), (), 0, length) for axis, length in enumerate(drawn.shape)]
        where[longest] = (where[longest] + shift) % drawn.shape[longest]
        spots.append(tuple(where))
    return drawn.at[spots[0]].set(least).at[spots[1]].set(high)


def block_scale(rng, shape, split, least, high):
    def one(position, shards_of):
        heights = jax.random.uniform(jax.random.fold_in(jax.random.fold_in(rng, 6), position), (shards_of,), jnp.float32, least / len(split), high / len(split))
        return jnp.repeat(jnp.exp(heights), shape[position] // shards_of).reshape((-1,) + (1,) * (len(shape) - position - 1))

    level = one(*split[0])
    for cut in split[1:]:
        level = level * one(*cut)
    return level


def setup_inputs(seed: int = 0) -> dict:
    splits = jax.random.split(jax.random.key(seed), 7)
    movie = jnp.clip(2.0 * jax.random.uniform(splits[0], (HEIGHT, WIDTH, FRAMES), jnp.float32) ** block_scale(splits[0], (HEIGHT, WIDTH, FRAMES), ((0, 2), (1, 16)), -0.2, 0.2), 0.0, 2.0).astype(jnp.bfloat16)
    footprints = jnp.clip(0.049804688 + 0.9501953 * jax.random.uniform(splits[1], (N_TY, N_TX, K_DEV, PATCH * PATCH), jnp.float32) ** block_scale(splits[1], (N_TY, N_TX, K_DEV, PATCH * PATCH), ((0, 2), (1, 16)), -0.2, 0.2), 0.049804688, 1.0).astype(jnp.bfloat16)
    centres = with_ends(jax.random.randint(splits[2], (N_TY, N_TX, K_DEV, 2), 0, TILE), jax.random.fold_in(splits[2], 1), 0, TILE - 1).astype(jnp.int32)
    traces = jnp.clip(1.0 * jax.random.uniform(splits[3], (N_TY, N_TX, K_DEV, FRAMES), jnp.float32) ** block_scale(splits[3], (N_TY, N_TX, K_DEV, FRAMES), ((0, 2), (1, 16)), -0.2, 0.2), 0.0, 1.0).astype(jnp.bfloat16)
    counts = with_ends(jax.random.randint(splits[4], (N_TY, N_TX), K_DEV // 4, K_DEV + 1), jax.random.fold_in(splits[4], 1), K_DEV // 4, K_DEV).astype(jnp.int32)
    order = jax.vmap(lambda own: jax.random.permutation(own, K_DEV))(jax.random.split(splits[5], N_TY * N_TX)).reshape((N_TY, N_TX, K_DEV)).astype(jnp.int32)
    return {"movie": movie, "footprints": footprints, "centres": centres, "traces": traces, "counts": counts, "order": order}


precise = lax.Precision.HIGHEST


def neighbours(values):
    rows_count = values.shape[0]
    cols_count = values.shape[1]
    widths = [(1, 1), (1, 1)] + [(0, 0)] * (values.ndim - 2)
    padded = jnp.pad(values, widths)
    pieces = [padded[step_down:step_down + rows_count, step_right:step_right + cols_count] for step_down in range(3) for step_right in range(3)]
    return jnp.stack(pieces, axis=2)


def by_order(values, ordering):
    index = ordering.reshape(ordering.shape + (1,) * (values.ndim - 3))
    return jnp.take_along_axis(values, index, axis=2)


def margin_rows(own_patch, own_rows, own_cols, source_patch, source_rows, source_cols):
    widened = jnp.pad(source_patch, ((0, 0), (PATCH, PATCH), (PATCH, PATCH)))

    def window_at(source_piece, source_row, source_col, row_at, col_at):
        first_row = jnp.clip(PATCH + row_at - source_row, 0, 2 * PATCH)
        first_col = jnp.clip(PATCH + col_at - source_col, 0, 2 * PATCH)
        return lax.dynamic_slice(source_piece, (first_row, first_col), (PATCH, PATCH))

    def against(row_at, col_at):
        return jax.vmap(window_at, in_axes=(0, 0, 0, None, None))(widened, source_rows, source_cols, row_at, col_at)

    windows = jax.vmap(against)(own_rows, own_cols)
    return jnp.einsum('kij,klij->kl', own_patch.astype(jnp.float32), windows.astype(jnp.float32), precision=precise)


def reference(movie, footprints, centres, traces, counts, order):
    tiles_down = counts.shape[0]
    tiles_across = counts.shape[1]
    slot_count = footprints.shape[2]
    tile_side = movie.shape[0] // tiles_down
    frame_count = movie.shape[2]
    half_patch = PATCH // 2
    block_rows = slot_count // BLOCKS
    alive_mask = order < counts[:, :, None]
    keep_mask = alive_mask.astype(jnp.bfloat16)
    patches = by_order(footprints, order) * keep_mask[..., None]
    patches = patches.reshape(tiles_down, tiles_across, slot_count, PATCH, PATCH)
    positions = by_order(centres, order)
    row_pos = positions[..., 0]
    col_pos = positions[..., 1]
    first_traces = by_order(traces, order) * keep_mask[..., None]

    padded_movie = jnp.pad(movie, ((half_patch, half_patch), (half_patch, half_patch), (0, 0)))
    top_rows = (jnp.arange(tiles_down, dtype=jnp.int32) * tile_side)[:, None, None] + row_pos
    left_cols = (jnp.arange(tiles_across, dtype=jnp.int32) * tile_side)[None, :, None] + col_pos

    def window_drive(patch, top_row, left_col):
        window = lax.dynamic_slice(padded_movie, (top_row, left_col, jnp.int32(0)), (PATCH, PATCH, frame_count))
        return jnp.einsum('ij,ijf->f', patch.astype(jnp.float32), window.astype(jnp.float32), precision=precise)

    def tile_drive(items):
        return jax.vmap(window_drive)(items[0], items[1], items[2])

    drive_term = lax.map(tile_drive, (patches.reshape(-1, slot_count, PATCH, PATCH), top_rows.reshape(-1, slot_count), left_cols.reshape(-1, slot_count)))
    drive_term = drive_term.reshape(tiles_down, tiles_across, slot_count, frame_count)

    offsets = (jnp.arange(3, dtype=jnp.int32) - 1) * tile_side
    near_patch = neighbours(patches)
    near_rows = neighbours(row_pos) + jnp.repeat(offsets, 3)[None, None, :, None]
    near_cols = neighbours(col_pos) + jnp.tile(offsets, 3)[None, None, :, None]

    def tile_margins(items):
        own_patch, own_rows, own_cols, source_patch, source_rows, source_cols = items

        def per_source(source_items):
            return margin_rows(own_patch, own_rows, own_cols, source_items[0], source_items[1], source_items[2])

        return lax.map(per_source, (source_patch, source_rows, source_cols))

    margins = lax.map(tile_margins, (patches.reshape(-1, slot_count, PATCH, PATCH), row_pos.reshape(-1, slot_count), col_pos.reshape(-1, slot_count), near_patch.reshape(-1, 9, slot_count, PATCH, PATCH), near_rows.reshape(-1, 9, slot_count), near_cols.reshape(-1, 9, slot_count)))
    margins = margins.reshape(tiles_down, tiles_across, 9, slot_count, slot_count)

    current = first_traces.astype(jnp.float32)
    coupling = jnp.einsum('abnks,abnsf->abkf', margins, neighbours(current), precision=precise)
    diagonal = jnp.diagonal(margins[:, :, 4], axis1=2, axis2=3)
    denominator = jnp.where(alive_mask, diagonal, 1.0)
    for block_index in range(BLOCKS):
        lower = block_index * block_rows
        upper = lower + block_rows
        previous = current[:, :, lower:upper]
        renewed = jnp.maximum(previous + (drive_term[:, :, lower:upper] - coupling[:, :, lower:upper]) / denominator[:, :, lower:upper, None], 0.0)
        renewed = jnp.where(alive_mask[:, :, lower:upper, None], renewed, 0.0)
        current = current.at[:, :, lower:upper].set(renewed)
        if block_index + 1 < BLOCKS:
            change = neighbours(renewed - previous)
            coupling = coupling + jnp.einsum('abnks,abnsf->abkf', margins[..., lower:upper], change, precision=precise)
    inverse = jnp.argsort(order, axis=2).astype(jnp.int32)
    return jnp.take_along_axis(current, inverse[..., None], axis=2)
```

```python
import functools

import jax
import jax.numpy as jnp
from jax import lax
from jax.experimental import pallas as pl
from jax.experimental.pallas import tpu as pltpu
from jax.sharding import PartitionSpec as P

BLOCKS = 4
PATCH = 32
LANES = 128


precise = lax.Precision.HIGHEST


def extended(x, sides, width):
    for axis, dim in sides:
        devices, length = (lax.axis_size(axis), x.shape[dim])
        up = [(i, (i + 1) % devices) for i in range(devices - 1)]
        down = [(j, i) for i, j in up]
        last = lax.slice_in_dim(x, length - width, length, axis=dim)
        first = lax.slice_in_dim(x, 0, width, axis=dim)
        before = lax.ppermute(last, axis, up)
        after = lax.ppermute(first, axis, down)
        x = jnp.concatenate([before, x, after], axis=dim)
    return x


def placement(anchors, extent, length):
    across = jnp.arange(extent, dtype=jnp.int32)[None, :, None]
    inside = jnp.arange(length, dtype=jnp.int32)[None, None, :]
    return (across == anchors[:, None, None] + inside).astype(jnp.bfloat16)


def paint(patches, top_rows, left_cols, canvas_rows, canvas_cols):
    rows_hot = placement(top_rows, canvas_rows, PATCH)
    cols_hot = placement(left_cols, canvas_cols, PATCH)
    spread = jnp.einsum(
        "kyi,kij->kyj", rows_hot, patches, preferred_element_type=jnp.float32
    ).astype(jnp.bfloat16)
    canvas = jnp.einsum(
        "kyj,kxj->kyx", spread, cols_hot, preferred_element_type=jnp.float32
    ).astype(jnp.bfloat16)
    return canvas.reshape(patches.shape[0], canvas_rows * canvas_cols)


def general_body(movie, footprints, centres, traces, counts, order):
    tile_side = movie.shape[0]
    frame_count = movie.shape[2]
    slot_count = footprints.shape[2]
    half_patch = PATCH // 2
    block_rows = slot_count // BLOCKS
    ordering = order[0, 0]
    alive_mask = ordering < counts[0, 0]
    selector = ordering[:, None] == jnp.arange(slot_count, dtype=jnp.int32)[None, :]
    chooser = (selector & alive_mask[:, None]).astype(jnp.bfloat16)
    own_flat = jnp.dot(chooser, footprints[0, 0], preferred_element_type=jnp.float32).astype(
        jnp.bfloat16
    )
    first_traces = jnp.dot(chooser, traces[0, 0], preferred_element_type=jnp.float32).astype(
        jnp.bfloat16
    )
    picker = selector.astype(jnp.int32)
    own_pos = jnp.sum(picker[:, :, None] * centres[0, 0][None, :, :], axis=1)
    near_flat, near_pos, near_traces = (
        extended(own_flat[None, None], (("ty", 0), ("tx", 1)), 1),
        extended(own_pos.astype(jnp.bfloat16)[None, None], (("ty", 0), ("tx", 1)), 1),
        extended(first_traces[None, None], (("ty", 0), ("tx", 1)), 1),
    )
    offsets = (jnp.arange(3, dtype=jnp.int32) - 1) * tile_side
    near_rows = (near_pos[..., 0].astype(jnp.int32) + offsets[:, None, None]).reshape(
        9 * slot_count
    )
    near_cols = (near_pos[..., 1].astype(jnp.int32) + offsets[None, :, None]).reshape(
        9 * slot_count
    )
    own_rows = own_pos[:, 0]
    own_cols = own_pos[:, 1]
    own_patch = own_flat.reshape(slot_count, PATCH, PATCH)
    near_patch = near_flat.reshape(9 * slot_count, PATCH, PATCH)
    canvas_side = tile_side + 2 * half_patch
    own_canvas = paint(own_patch, own_rows, own_cols, canvas_side, canvas_side)
    near_canvas = paint(near_patch, near_rows, near_cols, canvas_side, canvas_side)
    margins = lax.dot_general(
        own_canvas, near_canvas, (((1,), (1,)), ((), ())), preferred_element_type=jnp.float32
    )
    by_source = margins.reshape(slot_count, 9, slot_count)
    padded_movie = extended(movie, (("ty", 0), ("tx", 1)), half_patch)
    drive_term = jnp.dot(
        own_canvas,
        padded_movie.reshape(canvas_side * canvas_side, frame_count),
        preferred_element_type=jnp.float32,
    )
    current = first_traces.astype(jnp.float32)
    coupling = jnp.dot(
        margins,
        near_traces.reshape(9 * slot_count, frame_count).astype(jnp.float32),
        precision=precise,
        preferred_element_type=jnp.float32,
    )
    diagonal = jnp.diagonal(by_source[:, 4])
    denominator = jnp.where(alive_mask, diagonal, 1.0)
    for block_index in range(BLOCKS):
        lower = block_index * block_rows
        upper = lower + block_rows
        previous = current[lower:upper]
        renewed = jnp.maximum(
            previous
            + (drive_term[lower:upper] - coupling[lower:upper]) / denominator[lower:upper, None],
            0.0,
        )
        renewed = jnp.where(alive_mask[lower:upper, None], renewed, 0.0)
        current = current.at[lower:upper].set(renewed)
        if block_index + 1 < BLOCKS:
            change = extended((renewed - previous)[None, None], (("ty", 0), ("tx", 1)), 1)
            columns = by_source[:, :, lower:upper].reshape(slot_count, 9 * block_rows)
            coupling = coupling + jnp.dot(
                columns,
                change.reshape(9 * block_rows, frame_count),
                precision=precise,
                preferred_element_type=jnp.float32,
            )
    result = lax.dot_general(
        selector.astype(jnp.float32),
        current,
        (((0,), (0,)), ((), ())),
        precision=precise,
        preferred_element_type=jnp.float32,
    )
    return result[None, None]


def swap(x):
    return lax.ppermute(x, "ty", [(0, 1), (1, 0)])


def pairwise(x, step):
    count = lax.axis_size("tx")
    pairs = []
    for i in range(count - step):
        base = count * ((i // step) % 2)
        pairs += [(base + i, base + i + step), (base + i + step, base + i)]
    return lax.ppermute(x, ("ty", "tx"), pairs)


def upward(step):
    column = lax.axis_index("tx")
    return (((column // step) % 2) == lax.axis_index("ty")).astype(jnp.int32)


def near_kernel(
    slots, meta, own, direct, other, film_own, film_pair, film_direct, film_other,
    far1, far2, far3, keep, patches, trails, canvas, start, film,
):
    tiles = 6
    total = 6 * slots
    block = slots // BLOCKS
    group = 2 * block
    source = 3 * group
    pixels = PATCH * PATCH // LANES
    depth = canvas.shape[0] // total
    sources = ((own, 0), (own, 1), (direct, 0), (direct, 1), (other, 0), (other, 1))

    canvas[...] = jnp.zeros_like(canvas)
    for t, (ref, u) in enumerate(sources):
        rows = slots * pixels
        patches[t * rows:(t + 1) * rows, :] = ref[u, :rows, :].astype(jnp.float32)
        trails[t * slots:(t + 1) * slots, :] = ref[u, rows:rows + slots, :].astype(jnp.float32)

    lane = lax.broadcasted_iota(jnp.int32, (pixels, LANES), 1)
    sub = lax.broadcasted_iota(jnp.int32, (pixels, LANES), 0)
    low = lane < LANES // 2
    inner = lane & (LANES // 2 - 1)

    def paint(t, s):
        a = meta[t, 3 * slots + 1]
        j = meta[t, 3 * slots + 2]
        p = meta[t, s]
        live = (p < meta[t, 3 * slots]).astype(jnp.int32)
        top = a * PATCH + meta[t, slots + p]
        left = meta[t, 2 * slots + p] + (j - 1) * PATCH
        slot = (s // block) * source + j * group + a * block + s % block
        odd = top & 1
        level = top // 2
        value = patches[pl.ds(pl.multiple_of((t * slots + p) * pixels, pixels), pixels), :]
        shift = left + 32 * odd + LANES
        turned = [pltpu.roll(value, (shift + 32 * m) & (LANES - 1), 1) for m in range(4)]
        first = pltpu.roll(turned[0], odd, 0)
        inside = (inner >= left) & (inner < left + PATCH * live)
        even_rows = jnp.where(low, jnp.where(sub >= odd, first, 0.0), turned[1])
        odd_rows = jnp.where(low, turned[2], turned[3])
        last = jnp.where(inside & low & (sub < odd), first, 0.0)
        at = level * total + slot
        canvas[pl.ds(at, pixels, stride=2 * total), :] = jnp.where(inside, even_rows, 0.0)
        canvas[pl.ds(at + total, pixels, stride=2 * total), :] = jnp.where(inside, odd_rows, 0.0)
        canvas[pl.ds(at + 2 * pixels * total, 1), :] = last[0:1, :]
        trail = trails[pl.ds(t * slots + p, 1), :]
        start[pl.ds(slot, 1), :] = trail * live.astype(jnp.float32)

    for t in range(tiles):
        @pl.loop(0, slots // UNROLL)
        def _(step):
            for k in range(UNROLL):
                paint(t, step * UNROLL + k)

    height = film_own.shape[0]
    half = PATCH // 2
    row0 = pl.multiple_of(meta[0, 3 * slots + 1] * height, height)
    row1 = pl.multiple_of(meta[1, 3 * slots + 1] * height, height)
    film[pl.ds(row0, height), half:half + PATCH, :] = film_own[...]
    film[pl.ds(row1, height), half:half + PATCH, :] = film_pair[...]
    for t, ref in ((2, film_direct), (4, film_other)):
        for u in range(2):
            row = pl.multiple_of(meta[t + u, 3 * slots + 1] * height, height)
            part = ref[u * height:(u + 1) * height]
            side = meta[t + u, 3 * slots + 2]

            @pl.when(side == 0)
            def _():
                film[pl.ds(row, height), 0:half, :] = part

            @pl.when(side != 0)
            def _():
                film[pl.ds(row, height), half + PATCH:2 * PATCH, :] = part

    margins = jnp.zeros((2 * slots, total), jnp.float32)
    drive = jnp.zeros((2 * slots, film.shape[2]), jnp.float32)
    edge = half // 4
    for step in range(depth // 2):
        at = 2 * step * total
        painted = jnp.concatenate(
            [canvas[at:at + total, :], canvas[at + total:at + 2 * total, :]], axis=1
        ).astype(jnp.bfloat16)
        mine = jnp.concatenate(
            [painted[q * source + group:q * source + 2 * group] for q in range(BLOCKS)], axis=0
        )
        margins += lax.dot_general(
            mine, painted, (((1,), (1,)), ((), ())), preferred_element_type=jnp.float32
        )
        if edge <= step < depth // 2 - edge:
            pixels_here = film[(step - edge) * 4:(step - edge) * 4 + 4].reshape(2 * LANES, -1)
            drive += jnp.dot(mine, pixels_here, preferred_element_type=jnp.float32)

    coupling = jnp.dot(
        margins, start[...], precision=precise, preferred_element_type=jnp.float32
    )
    line = lax.broadcasted_iota(jnp.int32, margins.shape, 0)
    column = lax.broadcasted_iota(jnp.int32, margins.shape, 1)
    matching = column == (line // group) * source + group + line % group
    diagonal = jnp.sum(jnp.where(matching, margins, 0.0), axis=1, keepdims=True)
    diagonal = jnp.where(diagonal > 0.0, diagonal, 1.0)
    begin = jnp.concatenate(
        [start[q * source + group:q * source + 2 * group, :] for q in range(BLOCKS)], axis=0
    )
    level = begin + (drive - coupling) / diagonal
    share = margins / diagonal

    def rows_of(x, q):
        return x[q * group:(q + 1) * group]

    first = jnp.maximum(rows_of(level, 0), 0.0)
    change = first - rows_of(begin, 0)
    pieces = (
        change,
        rows_of(level, 1), rows_of(begin, 1), rows_of(share, 1)[:, :LANES],
        rows_of(level, 2), rows_of(begin, 2), rows_of(share, 2)[:, :LANES],
    )
    for ref in (far1, far2, far3):
        for i in range(ref.shape[0] // group):
            ref[i * group:(i + 1) * group, :] = pieces[i]
    keep[0:group, :] = first
    keep[group:2 * group, :] = rows_of(level, 3)
    keep[2 * group:3 * group, :] = rows_of(share, 3)[:, :LANES]
    keep[3 * group:4 * group, :total - LANES] = rows_of(share, 3)[:, LANES:]


def sweep_kernel(slots, where, mine, keep, direct, other, order, out, box, current):
    block = slots // BLOCKS
    group = 2 * block
    reach = BLOCKS - 1
    sizes = (7 * group, 4 * group, group)
    box[reach] = mine[...]
    at = 0
    for step in range(1, BLOCKS):
        size = sizes[step - 1]
        up = where[step]
        box[reach - step + 2 * step * up, 0:size, :] = direct[at:at + size, :]
        box[reach + step - 2 * step * up, 0:size, :] = other[at:at + size, :]
        at += size

    def exact(a, b):
        return jnp.dot(a, b, precision=precise, preferred_element_type=jnp.float32)

    def around(values, j):
        return [values[j - 1], values[j], values[j + 1]]

    def part(j, i):
        return box[j, i * group:(i + 1) * group, :]

    change0 = {j: part(j, 0) for j in range(2 * reach + 1)}
    renewed1, change1 = {}, {}
    for j in range(1, 2 * reach):
        near = jnp.concatenate(around(change0, j), axis=0)
        renewed1[j] = jnp.maximum(part(j, 1) - exact(part(j, 3)[:, :3 * group], near), 0.0)
        change1[j] = renewed1[j] - part(j, 2)
    renewed2, change2 = {}, {}
    for j in range(2, 2 * reach - 1):
        near = jnp.concatenate(around(change0, j) + around(change1, j), axis=0)
        renewed2[j] = jnp.maximum(part(j, 4) - exact(part(j, 6)[:, :6 * group], near), 0.0)
        change2[j] = renewed2[j] - part(j, 5)
    near = jnp.concatenate(
        around(change0, reach) + around(change1, reach) + around(change2, reach), axis=0
    )
    share = jnp.concatenate(
        [keep[2 * group:3 * group, :], keep[3 * group:4 * group, :9 * group - LANES]], axis=1
    )
    current[0:group, :] = keep[0:group, :]
    current[group:2 * group, :] = renewed1[reach]
    current[2 * group:3 * group, :] = renewed2[reach]
    current[3 * group:4 * group, :] = jnp.maximum(
        keep[group:2 * group, :] - exact(share, near), 0.0
    )
    row = pl.multiple_of(where[0] * block, block)
    ordered = jnp.concatenate(
        [current[pl.ds(q * group + row, block), :] for q in range(BLOCKS)], axis=0
    )
    place = lax.broadcasted_iota(jnp.int32, (slots, slots), 0) == order[...]
    out[...] = exact(place.astype(jnp.float32), ordered)


UNROLL = 4


def strip_body(movie, footprints, centres, traces, counts, order):
    height, width, frames = movie.shape
    slots = footprints.shape[2]
    half = PATCH // 2
    group = 2 * slots // BLOCKS
    bf16 = jnp.bfloat16
    core = lax.axis_index("ty")
    up = [upward(step) for step in range(1, BLOCKS)]

    numbers = jnp.concatenate(
        [order[0, 0], centres[0, 0, :, 0], centres[0, 0, :, 1], counts[0]]
    ).astype(bf16)
    numbers = jnp.pad(numbers[None], ((0, 15), (0, LANES - numbers.shape[0])))
    packed = jnp.concatenate(
        [footprints[0, 0].reshape(-1, LANES), traces[0, 0], numbers], axis=0
    )
    pair_packed = swap(packed)
    pair_movie = swap(movie)
    both = jnp.stack([packed, pair_packed])
    direct = pairwise(both, 1)
    edge = half * up[0]
    edges = jnp.concatenate(
        [
            lax.dynamic_slice_in_dim(movie, edge, half, axis=1),
            lax.dynamic_slice_in_dim(pair_movie, edge, half, axis=1),
        ],
        axis=0,
    )
    film_direct = pairwise(edges, 1)
    other = swap(direct)
    film_other = swap(film_direct)

    line = packed.shape[0] - 16
    meta = jnp.concatenate([both[:, line], direct[:, line], other[:, line]], axis=0)
    rows = jnp.stack([core, 1 - core, core, 1 - core, 1 - core, core])
    sides = jnp.stack([1, 1, 2 * up[0], 2 * up[0], 2 - 2 * up[0], 2 - 2 * up[0]])
    lanes = jnp.arange(LANES)[None]
    meta = jnp.where(
        lanes == 3 * slots + 1,
        rows[:, None],
        jnp.where(lanes == 3 * slots + 2, sides[:, None], meta.astype(jnp.int32)),
    ).astype(jnp.int32)

    vmem = pl.BlockSpec(memory_space=pltpu.VMEM)
    smem = pl.BlockSpec(memory_space=pltpu.SMEM)
    f32 = jnp.float32
    depth = (2 * height + PATCH) // 2
    far1, far2, far3, keep = pl.pallas_call(
        functools.partial(near_kernel, slots),
        out_shape=[
            jax.ShapeDtypeStruct((7 * group, frames), f32),
            jax.ShapeDtypeStruct((4 * group, frames), f32),
            jax.ShapeDtypeStruct((group, frames), f32),
            jax.ShapeDtypeStruct((4 * group, frames), f32),
        ],
        in_specs=[smem] + [vmem] * 7,
        out_specs=[vmem] * 4,
        scratch_shapes=[
            pltpu.VMEM((6 * slots * PATCH * PATCH // LANES, LANES), f32),
            pltpu.VMEM((6 * slots, frames), f32),
            pltpu.VMEM((depth * 6 * slots, LANES), f32),
            pltpu.VMEM((6 * slots, frames), f32),
            pltpu.VMEM((2 * height, 2 * PATCH, frames), bf16),
        ],
        name="near",
    )(meta, both, direct, other, movie, pair_movie, film_direct, film_other)

    far = jnp.concatenate([pairwise(far1, 1), pairwise(far2, 2), pairwise(far3, 3)], axis=0)
    far_other = swap(far)
    where = jnp.stack([core] + up).astype(jnp.int32)
    result = pl.pallas_call(
        functools.partial(sweep_kernel, slots),
        out_shape=jax.ShapeDtypeStruct((slots, frames), f32),
        in_specs=[smem] + [vmem] * 5,
        out_specs=vmem,
        scratch_shapes=[
            pltpu.VMEM((2 * BLOCKS - 1, 7 * group, frames), f32),
            pltpu.VMEM((4 * group, frames), f32),
        ],
        name="sweep",
    )(where, far1, keep, far, far_other, order[0])
    return result[None, None]


def body(movie, footprints, centres, traces, counts, order):
    strip = (
        lax.axis_size("ty") == 2
        and movie.shape == (PATCH, PATCH, LANES)
        and footprints.shape[2] == PATCH
    )
    chosen = strip_body if strip else general_body
    return chosen(movie, footprints, centres, traces, counts, order)


def solution(mesh):
    in_specs = (
        P("ty", "tx", None),
        P("ty", "tx", None, None),
        P("ty", "tx", None, None),
        P("ty", "tx", None, None),
        P("ty", "tx"),
        P("ty", "tx", None),
    )
    out_specs = P("ty", "tx", None, None)
    return jax.shard_map(body, mesh=mesh, in_specs=in_specs, out_specs=out_specs, check_vma=False)
```

```python
import jax
import jax.numpy as jnp
from jax import lax
from jax.experimental import pallas as pl
from jax.experimental.pallas import tpu as pltpu
from jax.sharding import PartitionSpec as P

BLOCKS = 4
PATCH = 32
LANES = 128


precise = lax.Precision.HIGHEST


def extended(x, sides, width):
    for axis, dim in sides:
        devices, length = (lax.axis_size(axis), x.shape[dim])
        up = [(i, (i + 1) % devices) for i in range(devices - 1)]
        down = [(j, i) for i, j in up]
        last = lax.slice_in_dim(x, length - width, length, axis=dim)
        first = lax.slice_in_dim(x, 0, width, axis=dim)
        before = lax.ppermute(last, axis, up)
        after = lax.ppermute(first, axis, down)
        x = jnp.concatenate([before, x, after], axis=dim)
    return x


def placement(anchors, extent, length):
    across = jnp.arange(extent, dtype=jnp.int32)[None, :, None]
    inside = jnp.arange(length, dtype=jnp.int32)[None, None, :]
    return (across == anchors[:, None, None] + inside).astype(jnp.bfloat16)


def paint(patches, top_rows, left_cols, canvas_rows, canvas_cols):
    rows_hot = placement(top_rows, canvas_rows, PATCH)
    cols_hot = placement(left_cols, canvas_cols, PATCH)
    spread = jnp.einsum(
        "kyi,kij->kyj", rows_hot, patches, preferred_element_type=jnp.float32
    ).astype(jnp.bfloat16)
    canvas = jnp.einsum(
        "kyj,kxj->kyx", spread, cols_hot, preferred_element_type=jnp.float32
    ).astype(jnp.bfloat16)
    return canvas.reshape(patches.shape[0], canvas_rows * canvas_cols)


def general_body(movie, footprints, centres, traces, counts, order):
    tile_side = movie.shape[0]
    frame_count = movie.shape[2]
    slot_count = footprints.shape[2]
    half_patch = PATCH // 2
    block_rows = slot_count // BLOCKS
    ordering = order[0, 0]
    alive_mask = ordering < counts[0, 0]
    selector = ordering[:, None] == jnp.arange(slot_count, dtype=jnp.int32)[None, :]
    chooser = (selector & alive_mask[:, None]).astype(jnp.bfloat16)
    own_flat = jnp.dot(chooser, footprints[0, 0], preferred_element_type=jnp.float32).astype(
        jnp.bfloat16
    )
    first_traces = jnp.dot(chooser, traces[0, 0], preferred_element_type=jnp.float32).astype(
        jnp.bfloat16
    )
    picker = selector.astype(jnp.int32)
    own_pos = jnp.sum(picker[:, :, None] * centres[0, 0][None, :, :], axis=1)
    near_flat, near_pos, near_traces = (
        extended(own_flat[None, None], (("ty", 0), ("tx", 1)), 1),
        extended(own_pos.astype(jnp.bfloat16)[None, None], (("ty", 0), ("tx", 1)), 1),
        extended(first_traces[None, None], (("ty", 0), ("tx", 1)), 1),
    )
    offsets = (jnp.arange(3, dtype=jnp.int32) - 1) * tile_side
    near_rows = (near_pos[..., 0].astype(jnp.int32) + offsets[:, None, None]).reshape(
        9 * slot_count
    )
    near_cols = (near_pos[..., 1].astype(jnp.int32) + offsets[None, :, None]).reshape(
        9 * slot_count
    )
    own_rows = own_pos[:, 0]
    own_cols = own_pos[:, 1]
    own_patch = own_flat.reshape(slot_count, PATCH, PATCH)
    near_patch = near_flat.reshape(9 * slot_count, PATCH, PATCH)
    canvas_side = tile_side + 2 * half_patch
    own_canvas = paint(own_patch, own_rows, own_cols, canvas_side, canvas_side)
    near_canvas = paint(near_patch, near_rows, near_cols, canvas_side, canvas_side)
    margins = lax.dot_general(
        own_canvas, near_canvas, (((1,), (1,)), ((), ())), preferred_element_type=jnp.float32
    )
    by_source = margins.reshape(slot_count, 9, slot_count)
    padded_movie = extended(movie, (("ty", 0), ("tx", 1)), half_patch)
    drive_term = jnp.dot(
        own_canvas,
        padded_movie.reshape(canvas_side * canvas_side, frame_count),
        preferred_element_type=jnp.float32,
    )
    current = first_traces.astype(jnp.float32)
    coupling = jnp.dot(
        margins,
        near_traces.reshape(9 * slot_count, frame_count).astype(jnp.float32),
        precision=precise,
        preferred_element_type=jnp.float32,
    )
    diagonal = jnp.diagonal(by_source[:, 4])
    denominator = jnp.where(alive_mask, diagonal, 1.0)
    for block_index in range(BLOCKS):
        lower = block_index * block_rows
        upper = lower + block_rows
        previous = current[lower:upper]
        renewed = jnp.maximum(
            previous
            + (drive_term[lower:upper] - coupling[lower:upper]) / denominator[lower:upper, None],
            0.0,
        )
        renewed = jnp.where(alive_mask[lower:upper, None], renewed, 0.0)
        current = current.at[lower:upper].set(renewed)
        if block_index + 1 < BLOCKS:
            change = extended((renewed - previous)[None, None], (("ty", 0), ("tx", 1)), 1)
            columns = by_source[:, :, lower:upper].reshape(slot_count, 9 * block_rows)
            coupling = coupling + jnp.dot(
                columns,
                change.reshape(9 * block_rows, frame_count),
                precision=precise,
                preferred_element_type=jnp.float32,
            )
    result = lax.dot_general(
        selector.astype(jnp.float32),
        current,
        (((0,), (0,)), ((), ())),
        precision=precise,
        preferred_element_type=jnp.float32,
    )
    return result[None, None]


OFFSETS = (
    ((-1, -3, 3, 1), (3, 1, -1, -3)),
    ((-2, -2, 2, 2), (-3, 3, -3, 3)),
    ((1, -1, 1, -1), (2, 2, -2, -2)),
)
BESIDE = ((1, -1, 1, -1), (-1, 1, -1, 1))
UNROLL = 4


def swap(x):
    return lax.ppermute(x, "ty", [(0, 1), (1, 0)])


def pairwise(x, offsets):
    count = lax.axis_size("tx")
    pairs = []
    for core, steps in enumerate(offsets):
        for i in range(count):
            other = i + steps[i % 4]
            if 0 <= other < count:
                pairs.append((core * count + i, core * count + other))
    return lax.ppermute(x, ("ty", "tx"), pairs)


def partner(offsets):
    core = lax.axis_index("ty")
    place = lax.axis_index("tx") & 3
    picked = []
    for steps in offsets:
        step = jnp.int32(steps[3])
        for i in range(3):
            step = jnp.where(place == i, steps[i], step)
        picked.append(step)
    return jnp.where(core == 0, picked[0], picked[1]), jnp.where(core == 0, picked[1], picked[0])


def pack_kernel(footprints, traces, order, centres, counts, packed, numbers):
    slots, width = footprints.shape
    numbers[...] = jnp.zeros_like(numbers)
    numbers[0:1, 0:slots] = order[...].astype(jnp.float32)
    numbers[1:3, 0:slots] = centres[...].astype(jnp.float32)
    numbers[3:4, 0:1] = counts[...].astype(jnp.float32)
    packed[:, :width] = footprints[...]
    packed[:, width:width + LANES] = traces[...]
    packed[:, width + LANES:] = numbers[...].astype(jnp.bfloat16)


def paint_kernel(
    own, direct, other, mine, links, scale, begin, coupling,
    patches, trails, canvas, start, numbers, meta, sem,
):
    slots = own.shape[1]
    tiles = 6
    total = tiles * slots
    block = slots // BLOCKS
    group = 2 * block
    source = 3 * group
    pixels = PATCH * PATCH // LANES
    width = pixels * LANES
    depth = canvas.shape[0] // total
    sources = ((own, 0), (own, 1), (direct, 0), (direct, 1), (other, 0), (other, 1))

    for t, (ref, u) in enumerate(sources):
        numbers[t * 8:(t + 1) * 8, :] = (
            ref[u, 0:16, width + LANES:].astype(jnp.float32)[0:8].astype(jnp.int32)
        )
    fetch = pltpu.make_async_copy(numbers, meta, sem)
    fetch.start()
    canvas[...] = jnp.zeros_like(canvas)
    for t, (ref, u) in enumerate(sources):
        for k in range(pixels):
            patches[pl.ds(t * slots * pixels + k, slots, stride=pixels), :] = ref[
                u, :, k * LANES:(k + 1) * LANES
            ].astype(jnp.float32)
        trails[t * slots:(t + 1) * slots, :] = ref[u, :, width:width + LANES].astype(jnp.float32)
    fetch.wait()

    lane = lax.broadcasted_iota(jnp.int32, (pixels, LANES), 1)
    sub = lax.broadcasted_iota(jnp.int32, (pixels, LANES), 0)
    low = lane < LANES // 2
    inner = lane & (LANES // 2 - 1)
    core = lax.axis_index("ty")
    step_direct, step_other = partner(BESIDE)
    tile_rows = (core, 1 - core, core, 1 - core, 1 - core, core)
    tile_cols = (0, 0, step_direct, step_direct, step_other, step_other)

    def paint(t, s):
        p = meta[t * 8, s]
        live = (p < meta[t * 8 + 3, 0]).astype(jnp.int32)
        top = tile_rows[t] * PATCH + meta[t * 8 + 1, p]
        left = meta[t * 8 + 2, p] + tile_cols[t] * PATCH
        slot = (
            (s // block) * source + (tile_cols[t] + 1) * group + tile_rows[t] * block + s % block
        )
        odd = top & 1
        level = top // 2
        value = patches[pl.ds(pl.multiple_of((t * slots + p) * pixels, pixels), pixels), :]
        shift = left + 32 * odd + LANES
        turned = [pltpu.roll(value, (shift + 32 * m) & (LANES - 1), 1) for m in range(4)]
        first = pltpu.roll(turned[0], odd, 0)
        inside = (inner >= left) & (inner < left + PATCH * live)
        even_rows = jnp.where(low, jnp.where(sub >= odd, first, 0.0), turned[1])
        odd_rows = jnp.where(low, turned[2], turned[3])
        last = jnp.where(inside & low & (sub < odd), first, 0.0)
        at = level * total + slot
        canvas[pl.ds(at, pixels, stride=2 * total), :] = jnp.where(inside, even_rows, 0.0)
        canvas[pl.ds(at + total, pixels, stride=2 * total), :] = jnp.where(inside, odd_rows, 0.0)
        canvas[pl.ds(at + 2 * pixels * total, 1), :] = last[0:1, :]
        trail = trails[pl.ds(t * slots + p, 1), :]
        start[pl.ds(slot, 1), :] = trail * live.astype(jnp.float32)

    for t in range(tiles):
        @pl.loop(0, slots // UNROLL)
        def _(step):
            for k in range(UNROLL):
                paint(t, step * UNROLL + k)

    margins = jnp.zeros((2 * slots, total), jnp.float32)
    edge = PATCH // 8
    for step in range(depth // 2):
        at = 2 * step * total
        painted = jnp.concatenate(
            [canvas[at:at + total, :], canvas[at + total:at + 2 * total, :]], axis=1
        ).astype(jnp.bfloat16)
        targets = jnp.concatenate(
            [painted[q * source + group:q * source + 2 * group] for q in range(BLOCKS)], axis=0
        )
        margins += lax.dot_general(
            targets, painted, (((1,), (1,)), ((), ())), preferred_element_type=jnp.float32
        )
        if edge <= step < depth // 2 - edge:
            mine[step - edge] = targets

    coupling[...] = jnp.dot(
        margins, start[...], precision=precise, preferred_element_type=jnp.float32
    )
    line = lax.broadcasted_iota(jnp.int32, margins.shape, 0)
    column = lax.broadcasted_iota(jnp.int32, margins.shape, 1)
    matching = column == (line // group) * source + group + line % group
    diagonal = jnp.sum(jnp.where(matching, margins, 0.0), axis=1, keepdims=True)
    diagonal = jnp.where(diagonal > 0.0, diagonal, 1.0)
    scale[...] = jnp.broadcast_to(diagonal, scale.shape)
    for q in range(BLOCKS):
        begin[q * group:(q + 1) * group, :] = start[q * source + group:q * source + 2 * group, :]
    share = margins / diagonal
    for i, q in enumerate((1, 2, 3)):
        links[i * group:(i + 1) * group, :] = share[q * group:(q + 1) * group, :LANES]
    links[3 * group:4 * group, :total - LANES] = share[3 * group:4 * group, LANES:]


def drive_kernel(
    mine, links, scale, begin, coupling, film_own, film_pair, film_direct, film_other,
    far, far_short, keep, film,
):
    core = lax.axis_index("ty")
    side_direct, side_other = partner(BESIDE)
    height = film_own.shape[0]
    half = PATCH // 2
    group = links.shape[0] // 4

    def row_of(a):
        return pl.ds(pl.multiple_of(a * height, height), height)

    film[row_of(core), half:half + PATCH, :] = film_own[...]
    film[row_of(1 - core), half:half + PATCH, :] = film_pair[...]
    for ref, side, nearest in ((film_direct, side_direct, core), (film_other, side_other, 1 - core)):
        for u in range(2):
            row = row_of(nearest if u == 0 else 1 - nearest)
            part = ref[u * height:(u + 1) * height]

            @pl.when(side < 0)
            def _():
                film[row, 0:half, :] = part

            @pl.when(side >= 0)
            def _():
                film[row, half + PATCH:2 * PATCH, :] = part

    drive = jnp.zeros(coupling.shape, jnp.float32)
    for step in range(mine.shape[0]):
        pixels_here = film[step * 4:(step + 1) * 4].reshape(mine.shape[2], -1)
        drive += jnp.dot(mine[step], pixels_here, preferred_element_type=jnp.float32)
    level = begin[...] + (drive - coupling[...]) / scale[...]

    def rows_of(x, q):
        return x[q * group:(q + 1) * group]

    first = jnp.maximum(rows_of(level, 0), 0.0)
    change = first - begin[0:group, :]
    pieces = (
        change,
        rows_of(level, 1), begin[group:2 * group, :], links[0:group, :],
        rows_of(level, 2), begin[2 * group:3 * group, :], links[group:2 * group, :],
    )
    for ref in (far, far_short):
        for i in range(ref.shape[0] // group):
            ref[i * group:(i + 1) * group, :] = pieces[i]
    keep[0:group, :] = first
    keep[group:2 * group, :] = rows_of(level, 3)
    keep[2 * group:4 * group, :] = links[2 * group:4 * group, :]


def sweep_kernel(mine, keep, direct, other, order, out, box, current):
    slots = out.shape[0]
    block = slots // BLOCKS
    group = 2 * block
    reach = BLOCKS - 1
    box[reach] = mine[...]
    at = 0
    for offsets, size in zip(OFFSETS, (7 * group, 4 * group, 7 * group)):
        step_direct, step_other = partner(offsets)
        box[reach + step_direct, 0:size, :] = direct[at:at + size, :]
        box[reach + step_other, 0:size, :] = other[at:at + size, :]
        at += size

    def exact(a, b):
        return jnp.dot(a, b, precision=precise, preferred_element_type=jnp.float32)

    def around(values, j):
        return [values[j - 1], values[j], values[j + 1]]

    def part(j, i):
        return box[j, i * group:(i + 1) * group, :]

    change0 = {j: part(j, 0) for j in range(2 * reach + 1)}
    renewed1, change1 = {}, {}
    for j in range(1, 2 * reach):
        near = jnp.concatenate(around(change0, j), axis=0)
        renewed1[j] = jnp.maximum(part(j, 1) - exact(part(j, 3)[:, :3 * group], near), 0.0)
        change1[j] = renewed1[j] - part(j, 2)
    renewed2, change2 = {}, {}
    for j in range(2, 2 * reach - 1):
        near = jnp.concatenate(around(change0, j) + around(change1, j), axis=0)
        renewed2[j] = jnp.maximum(part(j, 4) - exact(part(j, 6)[:, :6 * group], near), 0.0)
        change2[j] = renewed2[j] - part(j, 5)
    near = jnp.concatenate(
        around(change0, reach) + around(change1, reach) + around(change2, reach), axis=0
    )
    share = jnp.concatenate(
        [keep[2 * group:3 * group, :], keep[3 * group:4 * group, :9 * group - LANES]], axis=1
    )
    current[0:group, :] = keep[0:group, :]
    current[group:2 * group, :] = renewed1[reach]
    current[2 * group:3 * group, :] = renewed2[reach]
    current[3 * group:4 * group, :] = jnp.maximum(
        keep[group:2 * group, :] - exact(share, near), 0.0
    )
    row = pl.multiple_of(lax.axis_index("ty") * block, block)
    ordered = jnp.concatenate(
        [current[pl.ds(q * group + row, block), :] for q in range(BLOCKS)], axis=0
    )
    place = lax.broadcasted_iota(jnp.int32, (slots, slots), 0) == order[...]
    out[...] = exact(place.astype(jnp.float32), ordered)


def call(kernel, outs, scratch, megabytes, name):
    vmem = pl.BlockSpec(memory_space=pltpu.VMEM)

    def run(*operands):
        return pl.pallas_call(
            kernel,
            out_shape=[jax.ShapeDtypeStruct(*out) for out in outs],
            in_specs=[vmem] * len(operands),
            out_specs=[vmem] * len(outs),
            scratch_shapes=scratch,
            compiler_params=pltpu.CompilerParams(vmem_limit_bytes=megabytes << 20),
            name=name,
        )(*operands)

    return run


def strip_body(movie, footprints, centres, traces, counts, order):
    height, width, frames = movie.shape
    slots = footprints.shape[2]
    area = footprints.shape[3]
    half = PATCH // 2
    group = 2 * slots // BLOCKS
    total = 6 * slots
    bf16, f32 = jnp.bfloat16, jnp.float32

    pair_movie = swap(movie)
    (packed,) = call(
        pack_kernel,
        [((slots, area + 2 * LANES), bf16)],
        [pltpu.VMEM((slots, LANES), f32)],
        4,
        "pack",
    )(footprints[0, 0], traces[0, 0], order[0], centres[0, 0].T, counts)
    own = jnp.stack([packed, swap(packed)])
    direct = pairwise(own, BESIDE)
    edge = jnp.where(partner(BESIDE)[0] > 0, half, 0)
    edges = jnp.concatenate(
        [lax.dynamic_slice_in_dim(x, edge, half, axis=1) for x in (movie, pair_movie)], axis=0
    )
    film_direct = pairwise(edges, BESIDE)
    other = swap(direct)
    film_other = swap(film_direct)

    canvas_rows = (2 * height + PATCH) // 2
    painted = call(
        paint_kernel,
        [
            ((height // 2, 2 * slots, 2 * LANES), bf16),
            ((4 * group, LANES), f32),
            ((2 * slots, frames), f32),
            ((2 * slots, frames), f32),
            ((2 * slots, frames), f32),
        ],
        [
            pltpu.VMEM((total * area // LANES, LANES), f32),
            pltpu.VMEM((total, frames), f32),
            pltpu.VMEM((canvas_rows * total, LANES), f32),
            pltpu.VMEM((total, frames), f32),
            pltpu.VMEM((48, LANES), jnp.int32),
            pltpu.SMEM((48, LANES), jnp.int32),
            pltpu.SemaphoreType.DMA,
        ],
        16,
        "paint",
    )(own, direct, other)
    far, far_short, keep = call(
        drive_kernel,
        [((7 * group, frames), f32), ((4 * group, frames), f32), ((4 * group, frames), f32)],
        [pltpu.VMEM((2 * height, 2 * PATCH, frames), bf16)],
        8,
        "drive",
    )(*painted, movie, pair_movie, film_direct, film_other)

    came = jnp.concatenate(
        [
            pairwise(far, OFFSETS[0]),
            pairwise(far_short, OFFSETS[1]),
            pairwise(far, OFFSETS[2]),
        ],
        axis=0,
    )
    (result,) = call(
        sweep_kernel,
        [((slots, frames), f32)],
        [
            pltpu.VMEM((2 * BLOCKS - 1, 7 * group, frames), f32),
            pltpu.VMEM((4 * group, frames), f32),
        ],
        4,
        "sweep",
    )(far, keep, came, swap(came), order[0])
    return result[None, None]


def body(movie, footprints, centres, traces, counts, order):
    strip = (
        lax.axis_size("ty") == 2
        and movie.shape == (PATCH, PATCH, LANES)
        and footprints.shape[2] == PATCH
    )
    chosen = strip_body if strip else general_body
    return chosen(movie, footprints, centres, traces, counts, order)


def solution(mesh):
    in_specs = (
        P("ty", "tx", None),
        P("ty", "tx", None, None),
        P("ty", "tx", None, None),
        P("ty", "tx", None, None),
        P("ty", "tx"),
        P("ty", "tx", None),
    )
    out_specs = P("ty", "tx", None, None)
    return jax.shard_map(body, mesh=mesh, in_specs=in_specs, out_specs=out_specs, check_vma=False)
```

```python
import jax
import jax.numpy as jnp
from jax import lax
from jax.experimental import pallas as pl
from jax.experimental.pallas import tpu as pltpu
from jax.sharding import PartitionSpec as P

BLOCKS = 4
PATCH = 32
LANES = 128


precise = lax.Precision.HIGHEST


def extended(x, sides, width):
    for axis, dim in sides:
        devices, length = (lax.axis_size(axis), x.shape[dim])
        up = [(i, (i + 1) % devices) for i in range(devices - 1)]
        down = [(j, i) for i, j in up]
        last = lax.slice_in_dim(x, length - width, length, axis=dim)
        first = lax.slice_in_dim(x, 0, width, axis=dim)
        before = lax.ppermute(last, axis, up)
        after = lax.ppermute(first, axis, down)
        x = jnp.concatenate([before, x, after], axis=dim)
    return x


def placement(anchors, extent, length):
    across = jnp.arange(extent, dtype=jnp.int32)[None, :, None]
    inside = jnp.arange(length, dtype=jnp.int32)[None, None, :]
    return (across == anchors[:, None, None] + inside).astype(jnp.bfloat16)


def paint(patches, top_rows, left_cols, canvas_rows, canvas_cols):
    rows_hot = placement(top_rows, canvas_rows, PATCH)
    cols_hot = placement(left_cols, canvas_cols, PATCH)
    spread = jnp.einsum(
        "kyi,kij->kyj", rows_hot, patches, preferred_element_type=jnp.float32
    ).astype(jnp.bfloat16)
    canvas = jnp.einsum(
        "kyj,kxj->kyx", spread, cols_hot, preferred_element_type=jnp.float32
    ).astype(jnp.bfloat16)
    return canvas.reshape(patches.shape[0], canvas_rows * canvas_cols)


def general_body(movie, footprints, centres, traces, counts, order):
    tile_side = movie.shape[0]
    frame_count = movie.shape[2]
    slot_count = footprints.shape[2]
    half_patch = PATCH // 2
    block_rows = slot_count // BLOCKS
    ordering = order[0, 0]
    alive_mask = ordering < counts[0, 0]
    selector = ordering[:, None] == jnp.arange(slot_count, dtype=jnp.int32)[None, :]
    chooser = (selector & alive_mask[:, None]).astype(jnp.bfloat16)
    own_flat = jnp.dot(chooser, footprints[0, 0], preferred_element_type=jnp.float32).astype(
        jnp.bfloat16
    )
    first_traces = jnp.dot(chooser, traces[0, 0], preferred_element_type=jnp.float32).astype(
        jnp.bfloat16
    )
    picker = selector.astype(jnp.int32)
    own_pos = jnp.sum(picker[:, :, None] * centres[0, 0][None, :, :], axis=1)
    near_flat, near_pos, near_traces = (
        extended(own_flat[None, None], (("ty", 0), ("tx", 1)), 1),
        extended(own_pos.astype(jnp.bfloat16)[None, None], (("ty", 0), ("tx", 1)), 1),
        extended(first_traces[None, None], (("ty", 0), ("tx", 1)), 1),
    )
    offsets = (jnp.arange(3, dtype=jnp.int32) - 1) * tile_side
    near_rows = (near_pos[..., 0].astype(jnp.int32) + offsets[:, None, None]).reshape(
        9 * slot_count
    )
    near_cols = (near_pos[..., 1].astype(jnp.int32) + offsets[None, :, None]).reshape(
        9 * slot_count
    )
    own_rows = own_pos[:, 0]
    own_cols = own_pos[:, 1]
    own_patch = own_flat.reshape(slot_count, PATCH, PATCH)
    near_patch = near_flat.reshape(9 * slot_count, PATCH, PATCH)
    canvas_side = tile_side + 2 * half_patch
    own_canvas = paint(own_patch, own_rows, own_cols, canvas_side, canvas_side)
    near_canvas = paint(near_patch, near_rows, near_cols, canvas_side, canvas_side)
    margins = lax.dot_general(
        own_canvas, near_canvas, (((1,), (1,)), ((), ())), preferred_element_type=jnp.float32
    )
    by_source = margins.reshape(slot_count, 9, slot_count)
    padded_movie = extended(movie, (("ty", 0), ("tx", 1)), half_patch)
    drive_term = jnp.dot(
        own_canvas,
        padded_movie.reshape(canvas_side * canvas_side, frame_count),
        preferred_element_type=jnp.float32,
    )
    current = first_traces.astype(jnp.float32)
    coupling = jnp.dot(
        margins,
        near_traces.reshape(9 * slot_count, frame_count).astype(jnp.float32),
        precision=precise,
        preferred_element_type=jnp.float32,
    )
    diagonal = jnp.diagonal(by_source[:, 4])
    denominator = jnp.where(alive_mask, diagonal, 1.0)
    for block_index in range(BLOCKS):
        lower = block_index * block_rows
        upper = lower + block_rows
        previous = current[lower:upper]
        renewed = jnp.maximum(
            previous
            + (drive_term[lower:upper] - coupling[lower:upper]) / denominator[lower:upper, None],
            0.0,
        )
        renewed = jnp.where(alive_mask[lower:upper, None], renewed, 0.0)
        current = current.at[lower:upper].set(renewed)
        if block_index + 1 < BLOCKS:
            change = extended((renewed - previous)[None, None], (("ty", 0), ("tx", 1)), 1)
            columns = by_source[:, :, lower:upper].reshape(slot_count, 9 * block_rows)
            coupling = coupling + jnp.dot(
                columns,
                change.reshape(9 * block_rows, frame_count),
                precision=precise,
                preferred_element_type=jnp.float32,
            )
    result = lax.dot_general(
        selector.astype(jnp.float32),
        current,
        (((0,), (0,)), ((), ())),
        precision=precise,
        preferred_element_type=jnp.float32,
    )
    return result[None, None]


OFFSETS = (
    ((-1, -3, 3, 1), (3, 1, -1, -3)),
    ((-2, -2, 2, 2), (-3, 3, -3, 3)),
    ((1, -1, 1, -1), (2, 2, -2, -2)),
)
BESIDE = ((1, -1, 1, -1), (-1, 1, -1, 1))


def take_lanes(values, lanes):
    return jnp.take_along_axis(values, lanes, axis=1, mode="promise_in_bounds")


def swap(x):
    return lax.ppermute(x, "ty", [(0, 1), (1, 0)])


def pairwise(x, offsets):
    count = lax.axis_size("tx")
    pairs = []
    for core, steps in enumerate(offsets):
        for i in range(count):
            other = i + steps[i % 4]
            if 0 <= other < count:
                pairs.append((core * count + i, core * count + other))
    return lax.ppermute(x, ("ty", "tx"), pairs)


def partner(offsets):
    core = lax.axis_index("ty")
    place = lax.axis_index("tx") & 3
    picked = []
    for steps in offsets:
        step = jnp.int32(steps[3])
        for i in range(3):
            step = jnp.where(place == i, steps[i], step)
        picked.append(step)
    return jnp.where(core == 0, picked[0], picked[1]), jnp.where(core == 0, picked[1], picked[0])


def paint_kernel(
    own, direct, other, mine, links, scale, begin, coupling,
    patches, canvas, start, numbers, table, sem,
):
    slots = own.shape[1]
    tiles = 6
    total = tiles * slots
    block = slots // BLOCKS
    group = 2 * block
    source = 3 * group
    pixels = PATCH * PATCH // LANES
    width = pixels * LANES
    depth = canvas.shape[0] // total
    sources = ((own, 0), (own, 1), (direct, 0), (direct, 1), (other, 0), (other, 1))
    core = lax.axis_index("ty")
    step_direct, step_other = partner(BESIDE)
    tile_rows = (core, 1 - core, core, 1 - core, 1 - core, core)
    tile_cols = (0, 0, step_direct, step_direct, step_other, step_other)

    heads = [ref[u, 0:16, width + LANES:].astype(jnp.float32) for ref, u in sources]
    spare = [jnp.zeros((8 - tiles, LANES), jnp.float32)]
    ordering, top, left, count = (
        jnp.concatenate([head[i:i + 1, :] for head in heads] + spare, axis=0).astype(jnp.int32)
        for i in range(4)
    )
    row = lax.broadcasted_iota(jnp.int32, (8, LANES), 0)
    tile_row = jnp.zeros((8, LANES), jnp.int32)
    tile_col = jnp.zeros((8, LANES), jnp.int32)
    for t in range(tiles):
        tile_row = jnp.where(row == t, tile_rows[t], tile_row)
        tile_col = jnp.where(row == t, tile_cols[t], tile_col)
    slot_of = lax.broadcasted_iota(jnp.int32, (8, LANES), 1)
    live = (ordering < count[:, 0:1]).astype(jnp.int32)
    top = take_lanes(top, ordering) + tile_row * PATCH
    left = take_lanes(left, ordering) + tile_col * PATCH
    odd = top & 1
    spot = (
        lax.div(slot_of, block) * source
        + (tile_col + 1) * group
        + tile_row * block
        + lax.rem(slot_of, block)
        + lax.shift_right_logical(top, 1) * total
    )
    shift = left + 32 * odd
    fields = [(row * slots + ordering) * pixels, spot, left, left + PATCH * live, odd]
    fields += [(shift + 32 * m) & (LANES - 1) for m in range(4)]
    for i, field in enumerate(fields):
        numbers[i * 8:(i + 1) * 8, :] = field
    fetch = pltpu.make_async_copy(numbers, table, sem)
    fetch.start()

    canvas[...] = jnp.zeros_like(canvas)
    for t, (ref, u) in enumerate(sources):
        for k in range(pixels):
            patches[pl.ds(t * slots * pixels + k, slots, stride=pixels), :] = ref[
                u, :, k * LANES:(k + 1) * LANES
            ].astype(jnp.float32)
        which = lax.broadcasted_iota(jnp.int32, (slots, slots), 0)
        chosen = (which == ordering[t:t + 1, :slots]) & (which < count[t:t + 1, 0:1])
        trail = lax.dot_general(
            chosen.astype(jnp.bfloat16),
            ref[u, :, width:width + LANES],
            (((0,), (0,)), ((), ())),
            preferred_element_type=jnp.float32,
        )
        for q in range(BLOCKS):
            at = q * source + (tile_cols[t] + 1) * group + tile_rows[t] * block
            start[pl.ds(pl.multiple_of(at, block), block), :] = trail[q * block:(q + 1) * block]
    fetch.wait()

    lane = lax.broadcasted_iota(jnp.int32, (pixels, LANES), 1)
    sub = lax.broadcasted_iota(jnp.int32, (pixels, LANES), 0)
    low = lane < LANES // 2
    low_first = low & (sub == 0)
    inner = lane & (LANES // 2 - 1)

    def paint(t, s):
        origin, at, begins, ends, odd_row, *turns = (
            table[i * 8 + t, s] for i in range(len(fields))
        )
        value = patches[pl.ds(pl.multiple_of(origin, pixels), pixels), :]
        turned = [pltpu.roll(value, turn, 1) for turn in turns]
        down = pltpu.roll(turned[0], 1, 0)
        is_odd = jnp.broadcast_to(odd_row, sub.shape) > 0
        inside = (inner >= begins) & (inner < ends)
        first = jnp.where(is_odd, jnp.where(sub == 0, 0.0, down), turned[0])
        even_rows = jnp.where(low, first, turned[1])
        odd_rows = jnp.where(low, turned[2], turned[3])
        last = jnp.where(inside & low_first & is_odd, down, 0.0)
        canvas[pl.ds(at, pixels, stride=2 * total), :] = jnp.where(inside, even_rows, 0.0)
        canvas[pl.ds(at + total, pixels, stride=2 * total), :] = jnp.where(inside, odd_rows, 0.0)
        canvas[pl.ds(at + 2 * pixels * total, 1), :] = last[0:1, :]

    for t in range(tiles):
        for s in range(slots):
            paint(t, s)

    margins = jnp.zeros((2 * slots, total), jnp.float32)
    edge = PATCH // 8
    for step in range(depth // 2):
        at = 2 * step * total
        painted = jnp.concatenate(
            [canvas[at:at + total, :], canvas[at + total:at + 2 * total, :]], axis=1
        ).astype(jnp.bfloat16)
        targets = jnp.concatenate(
            [painted[q * source + group:q * source + 2 * group] for q in range(BLOCKS)], axis=0
        )
        margins += lax.dot_general(
            targets, painted, (((1,), (1,)), ((), ())), preferred_element_type=jnp.float32
        )
        if edge <= step < depth // 2 - edge:
            mine[step - edge] = targets

    coupling[...] = jnp.dot(
        margins, start[...], precision=precise, preferred_element_type=jnp.float32
    )
    line = lax.broadcasted_iota(jnp.int32, margins.shape, 0)
    column = lax.broadcasted_iota(jnp.int32, margins.shape, 1)
    matching = column == (line // group) * source + group + line % group
    diagonal = jnp.sum(jnp.where(matching, margins, 0.0), axis=1, keepdims=True)
    diagonal = jnp.where(diagonal > 0.0, diagonal, 1.0)
    scale[...] = jnp.broadcast_to(diagonal, scale.shape)
    for q in range(BLOCKS):
        begin[q * group:(q + 1) * group, :] = start[q * source + group:q * source + 2 * group, :]
    share = margins / diagonal
    for i, q in enumerate((1, 2, 3)):
        links[i * group:(i + 1) * group, :] = share[q * group:(q + 1) * group, :LANES]
    links[3 * group:4 * group, :total - LANES] = share[3 * group:4 * group, LANES:]


def drive_kernel(
    mine, links, scale, begin, coupling, film_own, film_pair, film_direct, film_other,
    far, far_short, keep, film,
):
    core = lax.axis_index("ty")
    side_direct, side_other = partner(BESIDE)
    height = film_own.shape[0]
    half = PATCH // 2
    group = links.shape[0] // 4

    def row_of(a):
        return pl.ds(pl.multiple_of(a * height, height), height)

    film[row_of(core), half:half + PATCH, :] = film_own[...]
    film[row_of(1 - core), half:half + PATCH, :] = film_pair[...]
    for ref, side, nearest in ((film_direct, side_direct, core), (film_other, side_other, 1 - core)):
        for u in range(2):
            row = row_of(nearest if u == 0 else 1 - nearest)
            part = ref[u * height:(u + 1) * height]

            @pl.when(side < 0)
            def _():
                film[row, 0:half, :] = part

            @pl.when(side >= 0)
            def _():
                film[row, half + PATCH:2 * PATCH, :] = part

    drive = jnp.zeros(coupling.shape, jnp.float32)
    for step in range(mine.shape[0]):
        pixels_here = film[step * 4:(step + 1) * 4].reshape(mine.shape[2], -1)
        drive += jnp.dot(mine[step], pixels_here, preferred_element_type=jnp.float32)
    level = begin[...] + (drive - coupling[...]) / scale[...]

    def rows_of(x, q):
        return x[q * group:(q + 1) * group]

    first = jnp.maximum(rows_of(level, 0), 0.0)
    change = first - begin[0:group, :]
    pieces = (
        change,
        rows_of(level, 1), begin[group:2 * group, :], links[0:group, :],
        rows_of(level, 2), begin[2 * group:3 * group, :], links[group:2 * group, :],
    )
    for ref in (far, far_short):
        for i in range(ref.shape[0] // group):
            ref[i * group:(i + 1) * group, :] = pieces[i]
    keep[0:group, :] = first
    keep[group:2 * group, :] = rows_of(level, 3)
    keep[2 * group:4 * group, :] = links[2 * group:4 * group, :]


def sweep_kernel(mine, keep, direct, other, order, out, box, current):
    slots = out.shape[0]
    block = slots // BLOCKS
    group = 2 * block
    reach = BLOCKS - 1
    box[reach] = mine[...]
    at = 0
    for offsets, size in zip(OFFSETS, (7 * group, 4 * group, 7 * group)):
        step_direct, step_other = partner(offsets)
        box[reach + step_direct, 0:size, :] = direct[at:at + size, :]
        box[reach + step_other, 0:size, :] = other[at:at + size, :]
        at += size

    def exact(a, b):
        return jnp.dot(a, b, precision=precise, preferred_element_type=jnp.float32)

    def around(values, j):
        return [values[j - 1], values[j], values[j + 1]]

    def part(j, i):
        return box[j, i * group:(i + 1) * group, :]

    change0 = {j: part(j, 0) for j in range(2 * reach + 1)}
    renewed1, change1 = {}, {}
    for j in range(1, 2 * reach):
        near = jnp.concatenate(around(change0, j), axis=0)
        renewed1[j] = jnp.maximum(part(j, 1) - exact(part(j, 3)[:, :3 * group], near), 0.0)
        change1[j] = renewed1[j] - part(j, 2)
    renewed2, change2 = {}, {}
    for j in range(2, 2 * reach - 1):
        near = jnp.concatenate(around(change0, j) + around(change1, j), axis=0)
        renewed2[j] = jnp.maximum(part(j, 4) - exact(part(j, 6)[:, :6 * group], near), 0.0)
        change2[j] = renewed2[j] - part(j, 5)
    near = jnp.concatenate(
        around(change0, reach) + around(change1, reach) + around(change2, reach), axis=0
    )
    share = jnp.concatenate(
        [keep[2 * group:3 * group, :], keep[3 * group:4 * group, :9 * group - LANES]], axis=1
    )
    current[0:group, :] = keep[0:group, :]
    current[group:2 * group, :] = renewed1[reach]
    current[2 * group:3 * group, :] = renewed2[reach]
    current[3 * group:4 * group, :] = jnp.maximum(
        keep[group:2 * group, :] - exact(share, near), 0.0
    )
    row = pl.multiple_of(lax.axis_index("ty") * block, block)
    ordered = jnp.concatenate(
        [current[pl.ds(q * group + row, block), :] for q in range(BLOCKS)], axis=0
    )
    place = lax.broadcasted_iota(jnp.int32, (slots, slots), 0) == order[...]
    out[...] = exact(place.astype(jnp.float32), ordered)


def call(kernel, outs, scratch, megabytes, space=pltpu.VMEM, cost=None):
    def run(*operands):
        return pl.pallas_call(
            kernel,
            out_shape=[jax.ShapeDtypeStruct(*out) for out in outs],
            in_specs=[pl.BlockSpec(memory_space=space)] * len(operands),
            out_specs=[pl.BlockSpec(memory_space=pltpu.VMEM)] * len(outs),
            scratch_shapes=scratch,
            compiler_params=pltpu.CompilerParams(vmem_limit_bytes=megabytes << 20),
            cost_estimate=cost,
        )(*operands)

    return run


def strip_body(movie, footprints, centres, traces, counts, order):
    height, _, frames = movie.shape
    slots = footprints.shape[2]
    area = footprints.shape[3]
    half = PATCH // 2
    group = 2 * slots // BLOCKS
    total = 6 * slots
    bf16, f32 = jnp.bfloat16, jnp.float32

    def spread(values, top):
        below = slots - top - values.shape[0]
        return jnp.pad(values, ((top, below), (0, LANES - values.shape[1])))

    numbers = spread(order[0], 0) + spread(centres[0, 0].T, 1) + spread(counts, 3)
    packed = jnp.concatenate(
        [footprints[0, 0], traces[0, 0], numbers.astype(bf16)], axis=1
    )
    film = movie
    own = jnp.stack([packed, swap(packed)])
    pair_film = swap(film)
    direct = pairwise(own, BESIDE)
    edge = jnp.where(partner(BESIDE)[0] > 0, half, 0)
    edges = jnp.concatenate(
        [lax.dynamic_slice_in_dim(x, edge, half, axis=1) for x in (film, pair_film)], axis=0
    )
    film_direct = pairwise(edges, BESIDE)
    other = swap(direct)
    film_other = swap(film_direct)

    canvas_rows = (2 * height + PATCH) // 2
    painted = call(
        paint_kernel,
        [
            ((height // 2, 2 * slots, 2 * LANES), bf16),
            ((4 * group, LANES), f32),
            ((2 * slots, frames), f32),
            ((2 * slots, frames), f32),
            ((2 * slots, frames), f32),
        ],
        [
            pltpu.VMEM((total * area // LANES, LANES), f32),
            pltpu.VMEM((canvas_rows * total, LANES), f32),
            pltpu.VMEM((total, frames), f32),
            pltpu.VMEM((72, LANES), jnp.int32),
            pltpu.SMEM((72, LANES), jnp.int32),
            pltpu.SemaphoreType.DMA,
        ],
        16,
        cost=pl.CostEstimate(flops=4_000_000_000, bytes_accessed=0, transcendentals=0),
    )(own, direct, other)
    far, far_short, keep = call(
        drive_kernel,
        [((7 * group, frames), f32), ((4 * group, frames), f32), ((4 * group, frames), f32)],
        [pltpu.VMEM((2 * height, 2 * PATCH, frames), bf16)],
        8,
    )(*painted, film, pair_film, film_direct, film_other)

    far0 = pairwise(far, OFFSETS[0])
    far1 = pairwise(far_short, OFFSETS[1])
    far2 = pairwise(far, OFFSETS[2])
    came = jnp.concatenate([far0, far1, far2], axis=0)
    (result,) = call(
        sweep_kernel,
        [((slots, frames), f32)],
        [
            pltpu.VMEM((2 * BLOCKS - 1, 7 * group, frames), f32),
            pltpu.VMEM((4 * group, frames), f32),
        ],
        4,
    )(far, keep, came, swap(came), order[0])
    return result[None, None]


def body(movie, footprints, centres, traces, counts, order):
    strip = (
        lax.axis_size("ty") == 2
        and movie.shape == (PATCH, PATCH, LANES)
        and footprints.shape[2] == PATCH
    )
    chosen = strip_body if strip else general_body
    return chosen(movie, footprints, centres, traces, counts, order)


def solution(mesh):
    in_specs = (
        P("ty", "tx", None),
        P("ty", "tx", None, None),
        P("ty", "tx", None, None),
        P("ty", "tx", None, None),
        P("ty", "tx"),
        P("ty", "tx", None),
    )
    out_specs = P("ty", "tx", None, None)
    return jax.shard_map(body, mesh=mesh, in_specs=in_specs, out_specs=out_specs, check_vma=False)
```

```python
import jax
import jax.numpy as jnp
from jax import lax
from jax.experimental import pallas as pl
from jax.experimental.pallas import tpu as pltpu
from jax.sharding import PartitionSpec as P

BLOCKS = 4
PATCH = 32
LANES = 128


precise = lax.Precision.HIGHEST


def extended(x, sides, width):
    for axis, dim in sides:
        devices, length = (lax.axis_size(axis), x.shape[dim])
        up = [(i, (i + 1) % devices) for i in range(devices - 1)]
        down = [(j, i) for i, j in up]
        last = lax.slice_in_dim(x, length - width, length, axis=dim)
        first = lax.slice_in_dim(x, 0, width, axis=dim)
        before = lax.ppermute(last, axis, up)
        after = lax.ppermute(first, axis, down)
        x = jnp.concatenate([before, x, after], axis=dim)
    return x


def placement(anchors, extent, length):
    across = jnp.arange(extent, dtype=jnp.int32)[None, :, None]
    inside = jnp.arange(length, dtype=jnp.int32)[None, None, :]
    return (across == anchors[:, None, None] + inside).astype(jnp.bfloat16)


def paint(patches, top_rows, left_cols, canvas_rows, canvas_cols):
    rows_hot = placement(top_rows, canvas_rows, PATCH)
    cols_hot = placement(left_cols, canvas_cols, PATCH)
    spread = jnp.einsum(
        "kyi,kij->kyj", rows_hot, patches, preferred_element_type=jnp.float32
    ).astype(jnp.bfloat16)
    canvas = jnp.einsum(
        "kyj,kxj->kyx", spread, cols_hot, preferred_element_type=jnp.float32
    ).astype(jnp.bfloat16)
    return canvas.reshape(patches.shape[0], canvas_rows * canvas_cols)


def general_body(movie, footprints, centres, traces, counts, order):
    tile_side = movie.shape[0]
    frame_count = movie.shape[2]
    slot_count = footprints.shape[2]
    half_patch = PATCH // 2
    block_rows = slot_count // BLOCKS
    ordering = order[0, 0]
    alive_mask = ordering < counts[0, 0]
    selector = ordering[:, None] == jnp.arange(slot_count, dtype=jnp.int32)[None, :]
    chooser = (selector & alive_mask[:, None]).astype(jnp.bfloat16)
    own_flat = jnp.dot(chooser, footprints[0, 0], preferred_element_type=jnp.float32).astype(
        jnp.bfloat16
    )
    first_traces = jnp.dot(chooser, traces[0, 0], preferred_element_type=jnp.float32).astype(
        jnp.bfloat16
    )
    picker = selector.astype(jnp.int32)
    own_pos = jnp.sum(picker[:, :, None] * centres[0, 0][None, :, :], axis=1)
    near_flat, near_pos, near_traces = (
        extended(own_flat[None, None], (("ty", 0), ("tx", 1)), 1),
        extended(own_pos.astype(jnp.bfloat16)[None, None], (("ty", 0), ("tx", 1)), 1),
        extended(first_traces[None, None], (("ty", 0), ("tx", 1)), 1),
    )
    offsets = (jnp.arange(3, dtype=jnp.int32) - 1) * tile_side
    near_rows = (near_pos[..., 0].astype(jnp.int32) + offsets[:, None, None]).reshape(
        9 * slot_count
    )
    near_cols = (near_pos[..., 1].astype(jnp.int32) + offsets[None, :, None]).reshape(
        9 * slot_count
    )
    own_rows = own_pos[:, 0]
    own_cols = own_pos[:, 1]
    own_patch = own_flat.reshape(slot_count, PATCH, PATCH)
    near_patch = near_flat.reshape(9 * slot_count, PATCH, PATCH)
    canvas_side = tile_side + 2 * half_patch
    own_canvas = paint(own_patch, own_rows, own_cols, canvas_side, canvas_side)
    near_canvas = paint(near_patch, near_rows, near_cols, canvas_side, canvas_side)
    margins = lax.dot_general(
        own_canvas, near_canvas, (((1,), (1,)), ((), ())), preferred_element_type=jnp.float32
    )
    by_source = margins.reshape(slot_count, 9, slot_count)
    padded_movie = extended(movie, (("ty", 0), ("tx", 1)), half_patch)
    drive_term = jnp.dot(
        own_canvas,
        padded_movie.reshape(canvas_side * canvas_side, frame_count),
        preferred_element_type=jnp.float32,
    )
    current = first_traces.astype(jnp.float32)
    coupling = jnp.dot(
        margins,
        near_traces.reshape(9 * slot_count, frame_count).astype(jnp.float32),
        precision=precise,
        preferred_element_type=jnp.float32,
    )
    diagonal = jnp.diagonal(by_source[:, 4])
    denominator = jnp.where(alive_mask, diagonal, 1.0)
    for block_index in range(BLOCKS):
        lower = block_index * block_rows
        upper = lower + block_rows
        previous = current[lower:upper]
        renewed = jnp.maximum(
            previous
            + (drive_term[lower:upper] - coupling[lower:upper]) / denominator[lower:upper, None],
            0.0,
        )
        renewed = jnp.where(alive_mask[lower:upper, None], renewed, 0.0)
        current = current.at[lower:upper].set(renewed)
        if block_index + 1 < BLOCKS:
            change = extended((renewed - previous)[None, None], (("ty", 0), ("tx", 1)), 1)
            columns = by_source[:, :, lower:upper].reshape(slot_count, 9 * block_rows)
            coupling = coupling + jnp.dot(
                columns,
                change.reshape(9 * block_rows, frame_count),
                precision=precise,
                preferred_element_type=jnp.float32,
            )
    result = lax.dot_general(
        selector.astype(jnp.float32),
        current,
        (((0,), (0,)), ((), ())),
        precision=precise,
        preferred_element_type=jnp.float32,
    )
    return result[None, None]


BESIDE = ((1, -1, 1, -1), (-1, 1, -1, 1))
EDGES = ((1, -1, 1, -1), (2, 2, -2, -2))
ACROSS = ((-1, -3, 3, 1), (3, 1, -1, -3))
PLANES = ((4, -4, 4, -4), (4, 4, -4, -4))
RELAYED = ((-3, 3, -3, 3), (-2, -2, 2, 2))


def take_lanes(values, lanes):
    return jnp.take_along_axis(values, lanes, axis=1, mode="promise_in_bounds")


def swap(x):
    return lax.ppermute(x, "ty", [(0, 1), (1, 0)])


def pairwise(x, offsets):
    count = lax.axis_size("tx")
    pairs = []
    for core, steps in enumerate(offsets):
        for i in range(count):
            other = i + steps[i % len(steps)]
            if 0 <= other < count:
                pairs.append((core * count + i, core * count + other))
    return lax.ppermute(x, ("ty", "tx"), pairs)


def partner(offsets):
    core = lax.axis_index("ty")
    picked = []
    for steps in offsets:
        place = lax.axis_index("tx") & (len(steps) - 1)
        step = jnp.int32(steps[-1])
        for i in range(len(steps) - 1):
            step = jnp.where(place == i, steps[i], step)
        picked.append(step)
    return jnp.where(core == 0, picked[0], picked[1]), jnp.where(core == 0, picked[1], picked[0])


def pack_kernel(
    counts, footprints, traces, order, centres,
    packed, ordering, patch_buf, trace_buf, order_buf, centre_buf, numbers, sems,
):
    pairs = (
        (order, order_buf),
        (centres, centre_buf),
        (footprints, patch_buf),
        (traces, trace_buf),
    )
    copies = [pltpu.make_async_copy(a, b, sems.at[i]) for i, (a, b) in enumerate(pairs)]
    for copy in copies:
        copy.start()
    slots, width = patch_buf.shape
    numbers[...] = jnp.zeros_like(numbers)
    for copy in copies:
        copy.wait()
    numbers[0:1, 0:slots] = order_buf[...].astype(jnp.float32)
    numbers[1:3, 0:slots] = centre_buf[...].astype(jnp.float32)
    numbers[3:4, :] = jnp.full((1, LANES), counts[0, 0], jnp.int32).astype(jnp.float32)
    ordering[...] = order_buf[...]
    packed[:, :width] = patch_buf[...]
    packed[:, width:width + LANES] = trace_buf[...]
    packed[:, width + LANES:] = numbers[...].astype(jnp.bfloat16)


def paint_kernel(
    own, direct, other, mine, links, scale, begin, coupling, beside,
    patches, canvas, start, numbers, table, sem,
):
    slots = own.shape[1]
    tiles = 6
    total = tiles * slots
    block = slots // BLOCKS
    group = 2 * block
    source = 3 * group
    pixels = PATCH * PATCH // LANES
    width = pixels * LANES
    depth = canvas.shape[0] // total
    sources = ((own, 0), (own, 1), (direct, 0), (direct, 1), (other, 0), (other, 1))
    core = lax.axis_index("ty")
    step_direct, step_other = partner(BESIDE)
    tile_rows = (core, 1 - core, core, 1 - core, 1 - core, core)
    tile_cols = (0, 0, step_direct, step_direct, step_other, step_other)

    heads = [ref[u, 0:16, width + LANES:].astype(jnp.float32) for ref, u in sources]
    spare = [jnp.zeros((8 - tiles, LANES), jnp.float32)]
    ordering, top, left, count = (
        jnp.concatenate([head[i:i + 1, :] for head in heads] + spare, axis=0).astype(jnp.int32)
        for i in range(4)
    )
    row = lax.broadcasted_iota(jnp.int32, (8, LANES), 0)
    tile_row = jnp.zeros((8, LANES), jnp.int32)
    tile_col = jnp.zeros((8, LANES), jnp.int32)
    for t in range(tiles):
        tile_row = jnp.where(row == t, tile_rows[t], tile_row)
        tile_col = jnp.where(row == t, tile_cols[t], tile_col)
    slot_of = lax.broadcasted_iota(jnp.int32, (8, LANES), 1)
    live = (ordering < count[:, 0:1]).astype(jnp.int32)
    top = take_lanes(top, ordering) + tile_row * PATCH
    left = take_lanes(left, ordering) + tile_col * PATCH
    odd = top & 1
    spot = (
        lax.div(slot_of, block) * source
        + (tile_col + 1) * group
        + tile_row * block
        + lax.rem(slot_of, block)
        + lax.shift_right_logical(top, 1) * total
    )
    shift = left + 32 * odd
    fields = [(row * slots + ordering) * pixels, spot, left, left + PATCH * live, odd]
    fields += [(shift + 32 * m) & (LANES - 1) for m in range(4)]
    for i, field in enumerate(fields):
        numbers[i * 8:(i + 1) * 8, :] = field
    fetch = pltpu.make_async_copy(numbers, table, sem)
    fetch.start()

    canvas[...] = jnp.zeros_like(canvas)
    for t, (ref, u) in enumerate(sources):
        for k in range(pixels):
            patches[pl.ds(t * slots * pixels + k, slots, stride=pixels), :] = ref[
                u, :, k * LANES:(k + 1) * LANES
            ].astype(jnp.float32)
        which = lax.broadcasted_iota(jnp.int32, (slots, slots), 0)
        chosen = (which == ordering[t:t + 1, :slots]) & (which < count[t:t + 1, 0:1])
        trail = lax.dot_general(
            chosen.astype(jnp.bfloat16),
            ref[u, :, width:width + LANES],
            (((0,), (0,)), ((), ())),
            preferred_element_type=jnp.float32,
        )
        for q in range(BLOCKS):
            at = q * source + (tile_cols[t] + 1) * group + tile_rows[t] * block
            start[pl.ds(pl.multiple_of(at, block), block), :] = trail[q * block:(q + 1) * block]
    fetch.wait()

    lane = lax.broadcasted_iota(jnp.int32, (pixels, LANES), 1)
    sub = lax.broadcasted_iota(jnp.int32, (pixels, LANES), 0)
    low = lane < LANES // 2
    low_first = low & (sub == 0)
    inner = lane & (LANES // 2 - 1)

    def paint(t, s):
        origin, at, begins, ends, odd_row, *turns = (
            table[i * 8 + t, s] for i in range(len(fields))
        )
        value = patches[pl.ds(pl.multiple_of(origin, pixels), pixels), :]
        turned = [pltpu.roll(value, turn, 1) for turn in turns]
        down = pltpu.roll(turned[0], 1, 0)
        is_odd = jnp.broadcast_to(odd_row, sub.shape) > 0
        inside = (inner >= begins) & (inner < ends)
        first = jnp.where(is_odd, jnp.where(sub == 0, 0.0, down), turned[0])
        even_rows = jnp.where(low, first, turned[1])
        odd_rows = jnp.where(low, turned[2], turned[3])
        last = jnp.where(inside & low_first & is_odd, down, 0.0)
        canvas[pl.ds(at, pixels, stride=2 * total), :] = jnp.where(inside, even_rows, 0.0)
        canvas[pl.ds(at + total, pixels, stride=2 * total), :] = jnp.where(inside, odd_rows, 0.0)
        canvas[pl.ds(at + 2 * pixels * total, 1), :] = last[0:1, :]

    for t in range(tiles):
        for s in range(slots):
            paint(t, s)

    margins = jnp.zeros((2 * slots, total), jnp.float32)
    edge = PATCH // 8
    for step in range(depth // 2):
        at = 2 * step * total
        painted = jnp.concatenate(
            [canvas[at:at + total, :], canvas[at + total:at + 2 * total, :]], axis=1
        ).astype(jnp.bfloat16)
        targets = jnp.concatenate(
            [painted[q * source + group:q * source + 2 * group] for q in range(BLOCKS)], axis=0
        )
        margins += lax.dot_general(
            targets, painted, (((1,), (1,)), ((), ())), preferred_element_type=jnp.float32
        )
        if edge <= step < depth // 2 - edge:
            mine[step - edge] = targets

    coupling[...] = jnp.dot(
        margins, start[...], precision=precise, preferred_element_type=jnp.float32
    )
    line = lax.broadcasted_iota(jnp.int32, margins.shape, 0)
    column = lax.broadcasted_iota(jnp.int32, margins.shape, 1)
    matching = column == (line // group) * source + group + line % group
    diagonal = jnp.sum(jnp.where(matching, margins, 0.0), axis=1, keepdims=True)
    diagonal = jnp.where(diagonal > 0.0, diagonal, 1.0)
    scale[...] = jnp.broadcast_to(diagonal, scale.shape)
    for q in range(BLOCKS):
        begin[q * group:(q + 1) * group, :] = start[q * source + group:q * source + 2 * group, :]
    for i, q in enumerate((1, 2)):
        for side in range(2):
            at = q * source + 2 * side * group
            beside[(2 * i + side) * group:(2 * i + side + 1) * group, :] = start[at:at + group, :]
    share = margins / diagonal
    for i, q in enumerate((1, 2, 3)):
        links[i * group:(i + 1) * group, :] = share[q * group:(q + 1) * group, :LANES]
    links[3 * group:4 * group, :total - LANES] = share[3 * group:4 * group, LANES:]


def drive_kernel(
    mine, links, scale, begin, coupling, film_own, film_pair, film_direct, film_other,
    near, across, level, film,
):
    core = lax.axis_index("ty")
    side_direct, side_other = partner(BESIDE)
    height = film_own.shape[0]
    half = PATCH // 2
    group = links.shape[0] // 4

    def row_of(a):
        return pl.ds(pl.multiple_of(a * height, height), height)

    film[row_of(core), half:half + PATCH, :] = film_own[...]
    film[row_of(1 - core), half:half + PATCH, :] = film_pair[...]
    for ref, side, nearest in ((film_direct, side_direct, core), (film_other, side_other, 1 - core)):
        for u in range(2):
            row = row_of(nearest if u == 0 else 1 - nearest)
            part = ref[u * height:(u + 1) * height]

            @pl.when(side < 0)
            def _():
                film[row, 0:half, :] = part

            @pl.when(side >= 0)
            def _():
                film[row, half + PATCH:2 * PATCH, :] = part

    drive = jnp.zeros(coupling.shape, jnp.float32)
    for step in range(mine.shape[0]):
        pixels_here = film[step * 4:(step + 1) * 4].reshape(mine.shape[2], -1)
        drive += jnp.dot(mine[step], pixels_here, preferred_element_type=jnp.float32)
    level[...] = begin[...] + (drive - coupling[...]) / scale[...]

    def rows_of(x, q):
        return x[q * group:(q + 1) * group, :]

    change = jnp.maximum(rows_of(level, 0), 0.0) - rows_of(begin, 0)
    varied = jnp.where(core == 0, rows_of(level, 2), rows_of(begin, 1))
    for ref, fourth in ((near, varied), (across, rows_of(level, 2))):
        pieces = (change, rows_of(level, 1), rows_of(links, 0), fourth, rows_of(links, 1))
        for i, piece in enumerate(pieces):
            ref[i * group:(i + 1) * group, :] = piece


def sweep_kernel(
    level, begin, links, beside, near_direct, near_other, across_direct, across_other,
    relay_direct, relay_other, order, out, box, current,
):
    slots = out.shape[0]
    block = slots // BLOCKS
    group = 2 * block
    reach = BLOCKS - 1
    refs = (near_direct, near_other, across_direct, across_other, relay_direct, relay_other)
    steps = (*partner(EDGES), *partner(ACROSS), *partner(RELAYED))
    for ref, step in zip(refs, steps):
        box[reach + step] = ref[...]

    def halves(x):
        high = x.astype(jnp.bfloat16)
        return high, (x - high.astype(jnp.float32)).astype(jnp.bfloat16)

    def product(a, b):
        (a1, a2), (b1, b2) = halves(a), halves(b)
        return sum(
            jnp.dot(x, y, preferred_element_type=jnp.float32)
            for x, y in ((a1, b1), (a1, b2), (a2, b1))
        )

    def block_of(x, i):
        return x[i * group:(i + 1) * group, :]

    def part(j, i):
        return box[j, i * group:(i + 1) * group, :]

    lane = lax.broadcasted_iota(jnp.int32, (group, LANES), 1)
    near = 3 * group

    def band(share, begins, target):
        kept = jnp.where((lane >= begins) & (lane < begins + near), share, 0.0)
        return pltpu.roll(kept, (target - begins) % LANES, 1)

    width = 2 * reach + 1
    spare = jnp.zeros((LANES - width * group, LANES), jnp.float32)
    first = jnp.maximum(block_of(level, 0), 0.0)
    change0 = [
        first - block_of(begin, 0) if j == reach else part(j, 0) for j in range(width)
    ]
    change0 = jnp.concatenate(change0 + [spare], axis=0)

    inner = range(1, width - 1)
    levels = [block_of(level, 1) if j == reach else part(j, 1) for j in inner]
    shares = [block_of(links, 0) if j == reach else part(j, 2) for j in inner]
    begins = [
        part(1, 3), block_of(beside, 0), block_of(begin, 1), block_of(beside, 1), part(5, 3)
    ]
    shares = [band(share, 0, (j - 1) * group) for j, share in zip(inner, shares)]
    renewed1 = jnp.maximum(
        jnp.concatenate(levels, axis=0) - product(jnp.concatenate(shares, axis=0), change0), 0.0
    )
    change1 = renewed1 - jnp.concatenate(begins, axis=0)
    spare = jnp.zeros((LANES - change1.shape[0], LANES), jnp.float32)
    changes = jnp.concatenate([change0, change1, spare], axis=0)

    inner = range(2, width - 2)
    levels = [block_of(level, 2) if j == reach else part(j, 3) for j in inner]
    shares = [block_of(links, 1) if j == reach else part(j, 4) for j in inner]
    begins = [block_of(beside, 2), block_of(begin, 2), block_of(beside, 3)]
    shares = [
        jnp.concatenate(
            [band(share, 0, (j - 1) * group), band(share, near, (j - 2) * group)], axis=1
        )
        for j, share in zip(inner, shares)
    ]
    renewed2 = jnp.maximum(
        jnp.concatenate(levels, axis=0) - product(jnp.concatenate(shares, axis=0), changes), 0.0
    )
    change2 = renewed2 - jnp.concatenate(begins, axis=0)

    middle = (reach - 1) * group
    changes = jnp.concatenate(
        [change0[middle:middle + near], change1[middle - group:middle - group + near], change2],
        axis=0,
    )
    share = jnp.concatenate([block_of(links, 2), block_of(links, 3)], axis=1)
    share = share[:, :3 * near]
    current[0:group, :] = first
    current[group:2 * group, :] = renewed1[middle:middle + group]
    current[2 * group:3 * group, :] = renewed2[group:2 * group]
    current[3 * group:4 * group, :] = jnp.maximum(
        block_of(level, 3) - product(share, changes), 0.0
    )
    row = pl.multiple_of(lax.axis_index("ty") * block, block)
    ordered = jnp.concatenate(
        [current[pl.ds(q * group + row, block), :] for q in range(BLOCKS)], axis=0
    )
    place = lax.broadcasted_iota(jnp.int32, (slots, slots), 0) == order[...]
    out[...] = jnp.dot(
        place.astype(jnp.float32), ordered, precision=precise, preferred_element_type=jnp.float32
    )


def call(kernel, outs, scratch, megabytes, spaces=None, cost=None):
    def run(*operands):
        return pl.pallas_call(
            kernel,
            out_shape=[jax.ShapeDtypeStruct(*out) for out in outs],
            in_specs=[
                pl.BlockSpec(memory_space=space)
                for space in spaces or [pltpu.VMEM] * len(operands)
            ],
            out_specs=[pl.BlockSpec(memory_space=pltpu.VMEM)] * len(outs),
            scratch_shapes=scratch,
            compiler_params=pltpu.CompilerParams(vmem_limit_bytes=megabytes << 20),
            cost_estimate=cost,
        )(*operands)

    return run


def strip_body(movie, footprints, centres, traces, counts, order):
    height, _, frames = movie.shape
    slots = footprints.shape[2]
    area = footprints.shape[3]
    half = PATCH // 2
    group = 2 * slots // BLOCKS
    total = 6 * slots
    bf16, f32 = jnp.bfloat16, jnp.float32

    given = (footprints[0, 0], traces[0, 0], order[0], centres[0, 0].T)
    packed, ordering = call(
        pack_kernel,
        [((slots, area + 2 * LANES), bf16), ((1, slots), jnp.int32)],
        [
            pltpu.VMEM((slots, area), bf16),
            pltpu.VMEM((slots, frames), bf16),
            pltpu.VMEM((1, slots), jnp.int32),
            pltpu.VMEM((2, slots), jnp.int32),
            pltpu.VMEM((slots, LANES), f32),
            pltpu.SemaphoreType.DMA((len(given),)),
        ],
        4,
        [pltpu.SMEM] + [pltpu.HBM] * len(given),
    )(counts, *(pltpu.with_memory_space_constraint(x, pltpu.HBM) for x in given))
    film = movie
    own = jnp.stack([packed, swap(packed)])
    pair_film = swap(film)
    direct = pairwise(own, BESIDE)
    edge = jnp.where(partner(BESIDE)[0] > 0, half, 0)
    edges = jnp.concatenate(
        [lax.dynamic_slice_in_dim(x, edge, half, axis=1) for x in (film, pair_film)], axis=0
    )
    film_direct = pairwise(edges, BESIDE)
    other = swap(direct)
    film_other = swap(film_direct)

    canvas_rows = (2 * height + PATCH) // 2
    painted = call(
        paint_kernel,
        [
            ((height // 2, 2 * slots, 2 * LANES), bf16),
            ((4 * group, LANES), f32),
            ((2 * slots, frames), f32),
            ((2 * slots, frames), f32),
            ((2 * slots, frames), f32),
            ((4 * group, frames), f32),
        ],
        [
            pltpu.VMEM((total * area // LANES, LANES), f32),
            pltpu.VMEM((canvas_rows * total, LANES), f32),
            pltpu.VMEM((total, frames), f32),
            pltpu.VMEM((72, LANES), jnp.int32),
            pltpu.SMEM((72, LANES), jnp.int32),
            pltpu.SemaphoreType.DMA,
        ],
        16,
        cost=pl.CostEstimate(flops=4_000_000_000, bytes_accessed=0, transcendentals=0),
    )(own, direct, other)
    mine, links, scale, begin, coupling, beside = painted
    near, across, level = call(
        drive_kernel,
        [((5 * group, frames), f32), ((5 * group, frames), f32), ((4 * group, frames), f32)],
        [pltpu.VMEM((2 * height, 2 * PATCH, frames), bf16)],
        8,
    )(mine, links, scale, begin, coupling, film, pair_film, film_direct, film_other)

    near_direct = pairwise(near, EDGES)
    across_direct = pairwise(across, ACROSS)
    relay_direct = pairwise(near_direct, PLANES)
    near_other = swap(near_direct)
    across_other = swap(across_direct)
    relay_other = swap(relay_direct)
    (result,) = call(
        sweep_kernel,
        [((slots, frames), f32)],
        [
            pltpu.VMEM((2 * BLOCKS - 1, 5 * group, frames), f32),
            pltpu.VMEM((4 * group, frames), f32),
        ],
        4,
    )(
        level, begin, links, beside, near_direct, near_other, across_direct, across_other,
        relay_direct, relay_other, ordering,
    )
    return result[None, None]


def body(movie, footprints, centres, traces, counts, order):
    strip = (
        lax.axis_size("ty") == 2
        and movie.shape == (PATCH, PATCH, LANES)
        and footprints.shape[2] == PATCH
    )
    chosen = strip_body if strip else general_body
    return chosen(movie, footprints, centres, traces, counts, order)


def solution(mesh):
    in_specs = (
        P("ty", "tx", None),
        P("ty", "tx", None, None),
        P("ty", "tx", None, None),
        P("ty", "tx", None, None),
        P("ty", "tx"),
        P("ty", "tx", None),
    )
    out_specs = P("ty", "tx", None, None)
    return jax.shard_map(body, mesh=mesh, in_specs=in_specs, out_specs=out_specs, check_vma=False)
```

```python
import jax
import jax.numpy as jnp
from jax import lax
from jax.experimental import pallas as pl
from jax.experimental.pallas import tpu as pltpu
from jax.sharding import PartitionSpec as P

BLOCKS = 4
PATCH = 32
LANES = 128


precise = lax.Precision.HIGHEST


def extended(x, sides, width):
    for axis, dim in sides:
        devices, length = (lax.axis_size(axis), x.shape[dim])
        up = [(i, (i + 1) % devices) for i in range(devices - 1)]
        down = [(j, i) for i, j in up]
        last = lax.slice_in_dim(x, length - width, length, axis=dim)
        first = lax.slice_in_dim(x, 0, width, axis=dim)
        before = lax.ppermute(last, axis, up)
        after = lax.ppermute(first, axis, down)
        x = jnp.concatenate([before, x, after], axis=dim)
    return x


def placement(anchors, extent, length):
    across = jnp.arange(extent, dtype=jnp.int32)[None, :, None]
    inside = jnp.arange(length, dtype=jnp.int32)[None, None, :]
    return (across == anchors[:, None, None] + inside).astype(jnp.bfloat16)


def paint(patches, top_rows, left_cols, canvas_rows, canvas_cols):
    rows_hot = placement(top_rows, canvas_rows, PATCH)
    cols_hot = placement(left_cols, canvas_cols, PATCH)
    spread = jnp.einsum(
        "kyi,kij->kyj", rows_hot, patches, preferred_element_type=jnp.float32
    ).astype(jnp.bfloat16)
    canvas = jnp.einsum(
        "kyj,kxj->kyx", spread, cols_hot, preferred_element_type=jnp.float32
    ).astype(jnp.bfloat16)
    return canvas.reshape(patches.shape[0], canvas_rows * canvas_cols)


def general_body(movie, footprints, centres, traces, counts, order):
    tile_side = movie.shape[0]
    frame_count = movie.shape[2]
    slot_count = footprints.shape[2]
    half_patch = PATCH // 2
    block_rows = slot_count // BLOCKS
    ordering = order[0, 0]
    alive_mask = ordering < counts[0, 0]
    selector = ordering[:, None] == jnp.arange(slot_count, dtype=jnp.int32)[None, :]
    chooser = (selector & alive_mask[:, None]).astype(jnp.bfloat16)
    own_flat = jnp.dot(chooser, footprints[0, 0], preferred_element_type=jnp.float32).astype(
        jnp.bfloat16
    )
    first_traces = jnp.dot(chooser, traces[0, 0], preferred_element_type=jnp.float32).astype(
        jnp.bfloat16
    )
    picker = selector.astype(jnp.int32)
    own_pos = jnp.sum(picker[:, :, None] * centres[0, 0][None, :, :], axis=1)
    near_flat, near_pos, near_traces = (
        extended(own_flat[None, None], (("ty", 0), ("tx", 1)), 1),
        extended(own_pos.astype(jnp.bfloat16)[None, None], (("ty", 0), ("tx", 1)), 1),
        extended(first_traces[None, None], (("ty", 0), ("tx", 1)), 1),
    )
    offsets = (jnp.arange(3, dtype=jnp.int32) - 1) * tile_side
    near_rows = (near_pos[..., 0].astype(jnp.int32) + offsets[:, None, None]).reshape(
        9 * slot_count
    )
    near_cols = (near_pos[..., 1].astype(jnp.int32) + offsets[None, :, None]).reshape(
        9 * slot_count
    )
    own_rows = own_pos[:, 0]
    own_cols = own_pos[:, 1]
    own_patch = own_flat.reshape(slot_count, PATCH, PATCH)
    near_patch = near_flat.reshape(9 * slot_count, PATCH, PATCH)
    canvas_side = tile_side + 2 * half_patch
    own_canvas = paint(own_patch, own_rows, own_cols, canvas_side, canvas_side)
    near_canvas = paint(near_patch, near_rows, near_cols, canvas_side, canvas_side)
    margins = lax.dot_general(
        own_canvas, near_canvas, (((1,), (1,)), ((), ())), preferred_element_type=jnp.float32
    )
    by_source = margins.reshape(slot_count, 9, slot_count)
    padded_movie = extended(movie, (("ty", 0), ("tx", 1)), half_patch)
    drive_term = jnp.dot(
        own_canvas,
        padded_movie.reshape(canvas_side * canvas_side, frame_count),
        preferred_element_type=jnp.float32,
    )
    current = first_traces.astype(jnp.float32)
    coupling = jnp.dot(
        margins,
        near_traces.reshape(9 * slot_count, frame_count).astype(jnp.float32),
        precision=precise,
        preferred_element_type=jnp.float32,
    )
    diagonal = jnp.diagonal(by_source[:, 4])
    denominator = jnp.where(alive_mask, diagonal, 1.0)
    for block_index in range(BLOCKS):
        lower = block_index * block_rows
        upper = lower + block_rows
        previous = current[lower:upper]
        renewed = jnp.maximum(
            previous
            + (drive_term[lower:upper] - coupling[lower:upper]) / denominator[lower:upper, None],
            0.0,
        )
        renewed = jnp.where(alive_mask[lower:upper, None], renewed, 0.0)
        current = current.at[lower:upper].set(renewed)
        if block_index + 1 < BLOCKS:
            change = extended((renewed - previous)[None, None], (("ty", 0), ("tx", 1)), 1)
            columns = by_source[:, :, lower:upper].reshape(slot_count, 9 * block_rows)
            coupling = coupling + jnp.dot(
                columns,
                change.reshape(9 * block_rows, frame_count),
                precision=precise,
                preferred_element_type=jnp.float32,
            )
    result = lax.dot_general(
        selector.astype(jnp.float32),
        current,
        (((0,), (0,)), ((), ())),
        precision=precise,
        preferred_element_type=jnp.float32,
    )
    return result[None, None]


EDGES = ((1, -1, 1, -1), (2, 2, -2, -2))
ACROSS = ((-1, -3, 3, 1), (3, 1, -1, -3))
PLANES = ((4, -4, 4, -4), (4, 4, -4, -4))
RELAYED = ((-3, 3, -3, 3), (-2, -2, 2, 2))


def take_lanes(values, lanes):
    return jnp.take_along_axis(values, lanes, axis=1, mode="promise_in_bounds")


def swap(x):
    return lax.ppermute(x, "ty", [(0, 1), (1, 0)])


def beside(x):
    count = lax.axis_size("tx")
    ring = list(range(count)) + list(range(2 * count - 1, count - 1, -1))
    return lax.ppermute(x, ("ty", "tx"), list(zip(ring, ring[1:] + ring[:1])))


def pairwise(x, offsets):
    count = lax.axis_size("tx")
    pairs = []
    for core, steps in enumerate(offsets):
        targets = [i + steps[i % len(steps)] for i in range(count)]
        used = [i for i in range(count) if 0 <= targets[i] < count]
        free = sorted(set(range(count)) - {targets[i] for i in used})
        idle = [i for i in range(count) if i not in used]
        if any(i == j for i, j in zip(idle, free)):
            free = [free[k ^ 1] if k ^ 1 < len(free) else free[k] for k in range(len(free))]
        for i, j in [(i, targets[i]) for i in used] + list(zip(idle, free)):
            pairs.append((core * count + i, core * count + j))
    return lax.ppermute(x, ("ty", "tx"), pairs)


def exists(step):
    column = lax.axis_index("tx") + step
    return (column >= 0) & (column < lax.axis_size("tx"))


def partner(offsets):
    core = lax.axis_index("ty")
    picked = []
    for steps in offsets:
        place = lax.axis_index("tx") & (len(steps) - 1)
        step = jnp.int32(steps[-1])
        for i in range(len(steps) - 1):
            step = jnp.where(place == i, steps[i], step)
        picked.append(step)
    return jnp.where(core == 0, picked[0], picked[1]), jnp.where(core == 0, picked[1], picked[0])


def pack_kernel(
    counts, footprints, traces, order, centres, movie,
    packed, ordering, film, patch_buf, trace_buf, order_buf, centre_buf, numbers, sems,
):
    pairs = (
        (order, order_buf),
        (centres, centre_buf),
        (footprints, patch_buf),
        (traces, trace_buf),
        (movie, film),
    )
    copies = [pltpu.make_async_copy(a, b, sems.at[i]) for i, (a, b) in enumerate(pairs)]
    for copy in copies:
        copy.start()
    slots, width = patch_buf.shape
    numbers[...] = jnp.zeros_like(numbers)
    for copy in copies[:4]:
        copy.wait()
    numbers[0:1, 0:slots] = order_buf[...].astype(jnp.float32)
    numbers[1:3, 0:slots] = centre_buf[...].astype(jnp.float32)
    numbers[3:4, :] = jnp.full((1, LANES), counts[0, 0], jnp.int32).astype(jnp.float32)
    ordering[...] = order_buf[...]
    packed[:, :width] = patch_buf[...]
    packed[:, width:width + LANES] = trace_buf[...]
    packed[:, width + LANES:] = numbers[...].astype(jnp.bfloat16)
    copies[4].wait()


def paint_tiles(
    sources, rows, columns, canvas, start, patches, numbers, table, sem, prepare=None
):
    slots = sources[0][0].shape[1]
    total = start.shape[0]
    block = slots // BLOCKS
    group = 2 * block
    source = 3 * group
    pixels = PATCH * PATCH // LANES
    width = pixels * LANES

    heads = [ref[u, 0:16, width + LANES:].astype(jnp.float32) for ref, u in sources]
    spare = [jnp.zeros((8 - len(sources), LANES), jnp.float32)]
    ordering, top, left, count = (
        jnp.concatenate([head[i:i + 1, :] for head in heads] + spare, axis=0).astype(jnp.int32)
        for i in range(4)
    )
    row = lax.broadcasted_iota(jnp.int32, (8, LANES), 0)
    tile_row = jnp.zeros((8, LANES), jnp.int32)
    tile_col = jnp.zeros((8, LANES), jnp.int32)
    for t in range(len(sources)):
        tile_row = jnp.where(row == t, rows[t], tile_row)
        tile_col = jnp.where(row == t, columns[t], tile_col)
        count = jnp.where((row == t) & jnp.logical_not(exists(columns[t])), 0, count)
    slot_of = lax.broadcasted_iota(jnp.int32, (8, LANES), 1)
    live = (ordering < count[:, 0:1]).astype(jnp.int32)
    top = take_lanes(top, ordering) + tile_row * PATCH
    left = take_lanes(left, ordering) + tile_col * PATCH
    odd = top & 1
    spot = (
        lax.div(slot_of, block) * source
        + (tile_col + 1) * group
        + tile_row * block
        + lax.rem(slot_of, block)
        + lax.shift_right_logical(top, 1) * total
    )
    shift = left + 32 * odd
    fields = [(row * slots + ordering) * pixels, spot, left, left + PATCH * live, odd]
    fields += [(shift + 32 * m) & (LANES - 1) for m in range(4)]
    for i, field in enumerate(fields):
        numbers[i * 8:(i + 1) * 8, :] = field
    fetch = pltpu.make_async_copy(numbers, table, sem)
    fetch.start()

    if prepare is not None:
        prepare()
    for t, (ref, u) in enumerate(sources):
        for k in range(pixels):
            patches[pl.ds(t * slots * pixels + k, slots, stride=pixels), :] = ref[
                u, :, k * LANES:(k + 1) * LANES
            ].astype(jnp.float32)
        which = lax.broadcasted_iota(jnp.int32, (slots, slots), 0)
        chosen = (which == ordering[t:t + 1, :slots]) & (which < count[t:t + 1, 0:1])
        trail = lax.dot_general(
            chosen.astype(jnp.bfloat16),
            ref[u, :, width:width + LANES],
            (((0,), (0,)), ((), ())),
            preferred_element_type=jnp.float32,
        )
        for q in range(BLOCKS):
            at = q * source + (columns[t] + 1) * group + rows[t] * block
            start[pl.ds(pl.multiple_of(at, block), block), :] = trail[q * block:(q + 1) * block]
    fetch.wait()

    lane = lax.broadcasted_iota(jnp.int32, (pixels, LANES), 1)
    sub = lax.broadcasted_iota(jnp.int32, (pixels, LANES), 0)
    low = lane < LANES // 2
    low_first = low & (sub == 0)
    inner = lane & (LANES // 2 - 1)

    for t in range(len(sources)):
        for s in range(slots):
            origin, at, begins, ends, odd_row, *turns = (
                table[i * 8 + t, s] for i in range(len(fields))
            )
            value = patches[pl.ds(pl.multiple_of(origin, pixels), pixels), :]
            turned = [pltpu.roll(value, turn, 1) for turn in turns]
            down = pltpu.roll(turned[0], 1, 0)
            is_odd = jnp.broadcast_to(odd_row, sub.shape) > 0
            inside = (inner >= begins) & (inner < ends)
            first = jnp.where(is_odd, jnp.where(sub == 0, 0.0, down), turned[0])
            even_rows = jnp.where(inside, jnp.where(low, first, turned[1]), 0.0)
            odd_rows = jnp.where(inside, jnp.where(low, turned[2], turned[3]), 0.0)
            last = jnp.where(inside & low_first & is_odd, down, 0.0)
            canvas[pl.ds(at, pixels, stride=2 * total), :] = even_rows
            canvas[pl.ds(at + total, pixels, stride=2 * total), :] = odd_rows
            canvas[pl.ds(at + 2 * pixels * total, 1), :] = last[0:1, :]


def own_kernel(own, canvas, start, patches, numbers, table, sem):
    core = lax.axis_index("ty")

    def clear():
        canvas[...] = jnp.zeros_like(canvas)

    paint_tiles(
        ((own, 0), (own, 1)), (core, 1 - core), (0, 0),
        canvas, start, patches, numbers, table, sem, clear,
    )


def near_kernel(
    canvas_own, start_own, direct, other,
    canvas, start, mine, links, scale, begin, coupling, begin_near,
    patches, numbers, table, sem,
):
    slots = direct.shape[1]
    total = start.shape[0]
    group = 2 * slots // BLOCKS
    source = 3 * group
    depth = canvas.shape[0] // total
    core = lax.axis_index("ty")
    step_direct = 2 * core - 1
    step_other = -step_direct
    paint_tiles(
        ((direct, 0), (direct, 1), (other, 0), (other, 1)),
        (core, 1 - core, 1 - core, core),
        (step_direct, step_direct, step_other, step_other),
        canvas, start, patches, numbers, table, sem,
    )

    margins = jnp.zeros((2 * slots, total), jnp.float32)
    edge = PATCH // 8
    for step in range(depth // 2):
        at = 2 * step * total
        painted = jnp.concatenate(
            [canvas[at:at + total, :], canvas[at + total:at + 2 * total, :]], axis=1
        ).astype(jnp.bfloat16)
        targets = jnp.concatenate(
            [painted[q * source + group:q * source + 2 * group] for q in range(BLOCKS)], axis=0
        )
        margins += lax.dot_general(
            targets, painted, (((1,), (1,)), ((), ())), preferred_element_type=jnp.float32
        )
        if edge <= step < depth // 2 - edge:
            mine[step - edge] = targets

    coupling[...] = jnp.dot(
        margins, start[...], precision=precise, preferred_element_type=jnp.float32
    )
    line = lax.broadcasted_iota(jnp.int32, margins.shape, 0)
    column = lax.broadcasted_iota(jnp.int32, margins.shape, 1)
    matching = column == (line // group) * source + group + line % group
    diagonal = jnp.sum(jnp.where(matching, margins, 0.0), axis=1, keepdims=True)
    diagonal = jnp.where(diagonal > 0.0, diagonal, 1.0)
    scale[...] = jnp.broadcast_to(diagonal, scale.shape)
    for q in range(BLOCKS):
        begin[q * group:(q + 1) * group, :] = start[q * source + group:q * source + 2 * group, :]
    for i, q in enumerate((1, 2)):
        for side in range(2):
            at = q * source + 2 * side * group
            row = (2 * i + side) * group
            begin_near[row:row + group, :] = start[at:at + group, :]
    share = margins / diagonal
    for i, q in enumerate((1, 2, 3)):
        links[i * group:(i + 1) * group, :] = share[q * group:(q + 1) * group, :LANES]
    links[3 * group:4 * group, :total - LANES] = share[3 * group:4 * group, LANES:]


def drive_kernel(
    mine, links, scale, begin, coupling, film_own, film_pair, film_direct, film_other,
    near, across, level, film,
):
    core = lax.axis_index("ty")
    side_direct = 2 * core - 1
    side_other = -side_direct
    height = film_own.shape[0]
    half = PATCH // 2
    group = links.shape[0] // 4

    def row_of(a):
        return pl.ds(pl.multiple_of(a * height, height), height)

    film[row_of(core), half:half + PATCH, :] = film_own[...]
    film[row_of(1 - core), half:half + PATCH, :] = film_pair[...]
    for ref, side, nearest in ((film_direct, side_direct, core), (film_other, side_other, 1 - core)):
        for u in range(2):
            row = row_of(nearest if u == 0 else 1 - nearest)
            part = ref[u * height:(u + 1) * height]
            part = jnp.where(exists(side), part, jnp.zeros_like(part))

            @pl.when(side < 0)
            def _():
                film[row, 0:half, :] = part

            @pl.when(side >= 0)
            def _():
                film[row, half + PATCH:2 * PATCH, :] = part

    drive = jnp.zeros(coupling.shape, jnp.float32)
    for step in range(mine.shape[0]):
        pixels_here = film[step * 4:(step + 1) * 4].reshape(mine.shape[2], -1)
        drive += jnp.dot(mine[step], pixels_here, preferred_element_type=jnp.float32)
    level[...] = begin[...] + (drive - coupling[...]) / scale[...]

    def rows_of(x, q):
        return x[q * group:(q + 1) * group, :]

    change = jnp.maximum(rows_of(level, 0), 0.0) - rows_of(begin, 0)
    varied = jnp.where(core == 0, rows_of(level, 2), rows_of(begin, 1))
    for ref, fourth in ((near, varied), (across, rows_of(level, 2))):
        pieces = (change, rows_of(level, 1), rows_of(links, 0), fourth, rows_of(links, 1))
        for i, piece in enumerate(pieces):
            ref[i * group:(i + 1) * group, :] = piece


def sweep_kernel(
    level, begin, links, begin_near, near_direct, near_other, across_direct, across_other,
    relay_direct, relay_other, order, out, box, current,
):
    slots = out.shape[0]
    block = slots // BLOCKS
    group = 2 * block
    reach = BLOCKS - 1
    refs = (near_direct, near_other, across_direct, across_other, relay_direct, relay_other)
    steps = (*partner(EDGES), *partner(ACROSS), *partner(RELAYED))
    for ref, step in zip(refs, steps):
        box[reach + step] = jnp.where(exists(step), ref[...], 0.0)

    def halves(x):
        high = x.astype(jnp.bfloat16)
        return high, (x - high.astype(jnp.float32)).astype(jnp.bfloat16)

    def product(a, b):
        (a1, a2), (b1, b2) = halves(a), halves(b)
        return sum(
            jnp.dot(x, y, preferred_element_type=jnp.float32)
            for x, y in ((a1, b1), (a1, b2), (a2, b1))
        )

    def block_of(x, i):
        return x[i * group:(i + 1) * group, :]

    def part(j, i):
        return box[j, i * group:(i + 1) * group, :]

    lane = lax.broadcasted_iota(jnp.int32, (group, LANES), 1)
    near = 3 * group

    def band(share, begins, target):
        kept = jnp.where((lane >= begins) & (lane < begins + near), share, 0.0)
        return pltpu.roll(kept, (target - begins) % LANES, 1)

    width = 2 * reach + 1
    spare = jnp.zeros((LANES - width * group, LANES), jnp.float32)
    first = jnp.maximum(block_of(level, 0), 0.0)
    change0 = [
        first - block_of(begin, 0) if j == reach else part(j, 0) for j in range(width)
    ]
    change0 = jnp.concatenate(change0 + [spare], axis=0)

    inner = range(1, width - 1)
    levels = [block_of(level, 1) if j == reach else part(j, 1) for j in inner]
    shares = [block_of(links, 0) if j == reach else part(j, 2) for j in inner]
    begins = [
        part(1, 3), block_of(begin_near, 0), block_of(begin, 1), block_of(begin_near, 1), part(5, 3)
    ]
    shares = [band(share, 0, (j - 1) * group) for j, share in zip(inner, shares)]
    renewed1 = jnp.maximum(
        jnp.concatenate(levels, axis=0) - product(jnp.concatenate(shares, axis=0), change0), 0.0
    )
    change1 = renewed1 - jnp.concatenate(begins, axis=0)
    spare = jnp.zeros((LANES - change1.shape[0], LANES), jnp.float32)
    changes = jnp.concatenate([change0, change1, spare], axis=0)

    inner = range(2, width - 2)
    levels = [block_of(level, 2) if j == reach else part(j, 3) for j in inner]
    shares = [block_of(links, 1) if j == reach else part(j, 4) for j in inner]
    begins = [block_of(begin_near, 2), block_of(begin, 2), block_of(begin_near, 3)]
    shares = [
        jnp.concatenate(
            [band(share, 0, (j - 1) * group), band(share, near, (j - 2) * group)], axis=1
        )
        for j, share in zip(inner, shares)
    ]
    renewed2 = jnp.maximum(
        jnp.concatenate(levels, axis=0) - product(jnp.concatenate(shares, axis=0), changes), 0.0
    )
    change2 = renewed2 - jnp.concatenate(begins, axis=0)

    middle = (reach - 1) * group
    changes = jnp.concatenate(
        [change0[middle:middle + near], change1[middle - group:middle - group + near], change2],
        axis=0,
    )
    share = jnp.concatenate([block_of(links, 2), block_of(links, 3)], axis=1)
    share = share[:, :3 * near]
    current[0:group, :] = first
    current[group:2 * group, :] = renewed1[middle:middle + group]
    current[2 * group:3 * group, :] = renewed2[group:2 * group]
    current[3 * group:4 * group, :] = jnp.maximum(
        block_of(level, 3) - product(share, changes), 0.0
    )
    row = pl.multiple_of(lax.axis_index("ty") * block, block)
    ordered = jnp.concatenate(
        [current[pl.ds(q * group + row, block), :] for q in range(BLOCKS)], axis=0
    )
    place = lax.broadcasted_iota(jnp.int32, (slots, slots), 0) == order[...]
    out[...] = jnp.dot(
        place.astype(jnp.float32), ordered, precision=precise, preferred_element_type=jnp.float32
    )


def call(kernel, outs, scratch, megabytes, spaces=None, cost=None, aliases={}):
    def run(*operands):
        return pl.pallas_call(
            kernel,
            out_shape=[jax.ShapeDtypeStruct(*out) for out in outs],
            in_specs=[
                pl.BlockSpec(memory_space=space)
                for space in spaces or [pltpu.VMEM] * len(operands)
            ],
            out_specs=[pl.BlockSpec(memory_space=pltpu.VMEM)] * len(outs),
            scratch_shapes=scratch,
            compiler_params=pltpu.CompilerParams(vmem_limit_bytes=megabytes << 20),
            cost_estimate=cost,
            input_output_aliases=aliases,
        )(*operands)

    return run


def strip_body(movie, footprints, centres, traces, counts, order):
    height, _, frames = movie.shape
    slots = footprints.shape[2]
    area = footprints.shape[3]
    half = PATCH // 2
    group = 2 * slots // BLOCKS
    total = 6 * slots
    bf16, f32 = jnp.bfloat16, jnp.float32

    given = (footprints[0, 0], traces[0, 0], order[0], centres[0, 0].T, movie)
    packed, ordering, film = call(
        pack_kernel,
        [((slots, area + 2 * LANES), bf16), ((1, slots), jnp.int32), (movie.shape, bf16)],
        [
            pltpu.VMEM((slots, area), bf16),
            pltpu.VMEM((slots, frames), bf16),
            pltpu.VMEM((1, slots), jnp.int32),
            pltpu.VMEM((2, slots), jnp.int32),
            pltpu.VMEM((slots, LANES), f32),
            pltpu.SemaphoreType.DMA((len(given),)),
        ],
        4,
        [pltpu.SMEM] + [pltpu.HBM] * len(given),
    )(counts, *(pltpu.with_memory_space_constraint(x, pltpu.HBM) for x in given))
    own = jnp.stack([packed, swap(packed)])
    pair_film = swap(film)
    direct = beside(own)
    edge = jnp.where(lax.axis_index("ty") == 0, half, 0)
    edges = jnp.concatenate(
        [lax.dynamic_slice_in_dim(x, edge, half, axis=1) for x in (film, pair_film)], axis=0
    )
    film_direct = beside(edges)
    other = swap(direct)
    film_other = swap(film_direct)

    canvas = ((2 * height + PATCH) // 2 * total, LANES)

    def painting(tiles):
        return [
            pltpu.VMEM((tiles * slots * area // LANES, LANES), f32),
            pltpu.VMEM((72, LANES), jnp.int32),
            pltpu.SMEM((72, LANES), jnp.int32),
            pltpu.SemaphoreType.DMA,
        ]

    own_canvas, own_start = call(
        own_kernel,
        [(canvas, f32), ((total, frames), f32)],
        painting(2),
        4,
        cost=pl.CostEstimate(flops=1_500_000_000, bytes_accessed=0, transcendentals=0),
    )(own)
    *_, mine, links, scale, begin, coupling, begin_near = call(
        near_kernel,
        [
            (canvas, f32),
            ((total, frames), f32),
            ((height // 2, 2 * slots, 2 * LANES), bf16),
            ((4 * group, LANES), f32),
            ((2 * slots, frames), f32),
            ((2 * slots, frames), f32),
            ((2 * slots, frames), f32),
            ((4 * group, frames), f32),
        ],
        painting(4),
        8,
        cost=pl.CostEstimate(flops=3_000_000_000, bytes_accessed=0, transcendentals=0),
        aliases={0: 0, 1: 1},
    )(own_canvas, own_start, direct, other)
    near, across, level = call(
        drive_kernel,
        [((5 * group, frames), f32), ((5 * group, frames), f32), ((4 * group, frames), f32)],
        [pltpu.VMEM((2 * height, 2 * PATCH, frames), bf16)],
        8,
    )(mine, links, scale, begin, coupling, film, pair_film, film_direct, film_other)

    near_direct = pairwise(near, EDGES)
    across_direct = pairwise(across, ACROSS)
    relay_direct = pairwise(near_direct, PLANES)
    near_other = swap(near_direct)
    across_other = swap(across_direct)
    relay_other = swap(relay_direct)
    (result,) = call(
        sweep_kernel,
        [((slots, frames), f32)],
        [
            pltpu.VMEM((2 * BLOCKS - 1, 5 * group, frames), f32),
            pltpu.VMEM((4 * group, frames), f32),
        ],
        4,
    )(
        level, begin, links, begin_near, near_direct, near_other, across_direct, across_other,
        relay_direct, relay_other, ordering,
    )
    return result[None, None]


def body(movie, footprints, centres, traces, counts, order):
    strip = (
        lax.axis_size("ty") == 2
        and movie.shape == (PATCH, PATCH, LANES)
        and footprints.shape[2] == PATCH
    )
    chosen = strip_body if strip else general_body
    return chosen(movie, footprints, centres, traces, counts, order)


def solution(mesh):
    in_specs = (
        P("ty", "tx", None),
        P("ty", "tx", None, None),
        P("ty", "tx", None, None),
        P("ty", "tx", None, None),
        P("ty", "tx"),
        P("ty", "tx", None),
    )
    out_specs = P("ty", "tx", None, None)
    return jax.shard_map(body, mesh=mesh, in_specs=in_specs, out_specs=out_specs, check_vma=False)
```

```python
import jax
import jax.numpy as jnp
from jax import lax
from jax.experimental import pallas as pl
from jax.experimental.pallas import tpu as pltpu
from jax.sharding import PartitionSpec as P

BLOCKS = 4
PATCH = 32
LANES = 128


precise = lax.Precision.HIGHEST


def extended(x, sides, width):
    for axis, dim in sides:
        devices, length = (lax.axis_size(axis), x.shape[dim])
        up = [(i, (i + 1) % devices) for i in range(devices - 1)]
        down = [(j, i) for i, j in up]
        last = lax.slice_in_dim(x, length - width, length, axis=dim)
        first = lax.slice_in_dim(x, 0, width, axis=dim)
        before = lax.ppermute(last, axis, up)
        after = lax.ppermute(first, axis, down)
        x = jnp.concatenate([before, x, after], axis=dim)
    return x


def placement(anchors, extent, length):
    across = jnp.arange(extent, dtype=jnp.int32)[None, :, None]
    inside = jnp.arange(length, dtype=jnp.int32)[None, None, :]
    return (across == anchors[:, None, None] + inside).astype(jnp.bfloat16)


def paint(patches, top_rows, left_cols, canvas_rows, canvas_cols):
    rows_hot = placement(top_rows, canvas_rows, PATCH)
    cols_hot = placement(left_cols, canvas_cols, PATCH)
    spread = jnp.einsum(
        "kyi,kij->kyj", rows_hot, patches, preferred_element_type=jnp.float32
    ).astype(jnp.bfloat16)
    canvas = jnp.einsum(
        "kyj,kxj->kyx", spread, cols_hot, preferred_element_type=jnp.float32
    ).astype(jnp.bfloat16)
    return canvas.reshape(patches.shape[0], canvas_rows * canvas_cols)


def general_body(movie, footprints, centres, traces, counts, order):
    tile_side = movie.shape[0]
    frame_count = movie.shape[2]
    slot_count = footprints.shape[2]
    half_patch = PATCH // 2
    block_rows = slot_count // BLOCKS
    ordering = order[0, 0]
    alive_mask = ordering < counts[0, 0]
    selector = ordering[:, None] == jnp.arange(slot_count, dtype=jnp.int32)[None, :]
    chooser = (selector & alive_mask[:, None]).astype(jnp.bfloat16)
    own_flat = jnp.dot(chooser, footprints[0, 0], preferred_element_type=jnp.float32).astype(
        jnp.bfloat16
    )
    first_traces = jnp.dot(chooser, traces[0, 0], preferred_element_type=jnp.float32).astype(
        jnp.bfloat16
    )
    picker = selector.astype(jnp.int32)
    own_pos = jnp.sum(picker[:, :, None] * centres[0, 0][None, :, :], axis=1)
    near_flat, near_pos, near_traces = (
        extended(own_flat[None, None], (("ty", 0), ("tx", 1)), 1),
        extended(own_pos.astype(jnp.bfloat16)[None, None], (("ty", 0), ("tx", 1)), 1),
        extended(first_traces[None, None], (("ty", 0), ("tx", 1)), 1),
    )
    offsets = (jnp.arange(3, dtype=jnp.int32) - 1) * tile_side
    near_rows = (near_pos[..., 0].astype(jnp.int32) + offsets[:, None, None]).reshape(
        9 * slot_count
    )
    near_cols = (near_pos[..., 1].astype(jnp.int32) + offsets[None, :, None]).reshape(
        9 * slot_count
    )
    own_rows = own_pos[:, 0]
    own_cols = own_pos[:, 1]
    own_patch = own_flat.reshape(slot_count, PATCH, PATCH)
    near_patch = near_flat.reshape(9 * slot_count, PATCH, PATCH)
    canvas_side = tile_side + 2 * half_patch
    own_canvas = paint(own_patch, own_rows, own_cols, canvas_side, canvas_side)
    near_canvas = paint(near_patch, near_rows, near_cols, canvas_side, canvas_side)
    margins = lax.dot_general(
        own_canvas, near_canvas, (((1,), (1,)), ((), ())), preferred_element_type=jnp.float32
    )
    by_source = margins.reshape(slot_count, 9, slot_count)
    padded_movie = extended(movie, (("ty", 0), ("tx", 1)), half_patch)
    drive_term = jnp.dot(
        own_canvas,
        padded_movie.reshape(canvas_side * canvas_side, frame_count),
        preferred_element_type=jnp.float32,
    )
    current = first_traces.astype(jnp.float32)
    coupling = jnp.dot(
        margins,
        near_traces.reshape(9 * slot_count, frame_count).astype(jnp.float32),
        precision=precise,
        preferred_element_type=jnp.float32,
    )
    diagonal = jnp.diagonal(by_source[:, 4])
    denominator = jnp.where(alive_mask, diagonal, 1.0)
    for block_index in range(BLOCKS):
        lower = block_index * block_rows
        upper = lower + block_rows
        previous = current[lower:upper]
        renewed = jnp.maximum(
            previous
            + (drive_term[lower:upper] - coupling[lower:upper]) / denominator[lower:upper, None],
            0.0,
        )
        renewed = jnp.where(alive_mask[lower:upper, None], renewed, 0.0)
        current = current.at[lower:upper].set(renewed)
        if block_index + 1 < BLOCKS:
            change = extended((renewed - previous)[None, None], (("ty", 0), ("tx", 1)), 1)
            columns = by_source[:, :, lower:upper].reshape(slot_count, 9 * block_rows)
            coupling = coupling + jnp.dot(
                columns,
                change.reshape(9 * block_rows, frame_count),
                precision=precise,
                preferred_element_type=jnp.float32,
            )
    result = lax.dot_general(
        selector.astype(jnp.float32),
        current,
        (((0,), (0,)), ((), ())),
        precision=precise,
        preferred_element_type=jnp.float32,
    )
    return result[None, None]


EDGES = ((1, -1, 1, -1), (2, 2, -2, -2))
ACROSS = ((-1, -3, 3, 1), (3, 1, -1, -3))
CROSS = ((-2, -2, 2, 2), (-3, 3, -3, 3))


def take_lanes(values, lanes):
    return jnp.take_along_axis(values, lanes, axis=1, mode="promise_in_bounds")


def swap(x):
    return lax.ppermute(x, "ty", [(0, 1), (1, 0)])


def beside(x, turn=1):
    count = lax.axis_size("tx")
    ring = list(range(count)) + list(range(2 * count - 1, count - 1, -1))
    ring = ring[::turn]
    return lax.ppermute(x, ("ty", "tx"), list(zip(ring, ring[1:] + ring[:1])))


def pairwise(x, offsets):
    count = lax.axis_size("tx")
    pairs = []
    for core, steps in enumerate(offsets):
        targets = [i + steps[i % len(steps)] for i in range(count)]
        used = [i for i in range(count) if 0 <= targets[i] < count]
        free = sorted(set(range(count)) - {targets[i] for i in used})
        idle = [i for i in range(count) if i not in used]
        if any(i == j for i, j in zip(idle, free)):
            free = [free[k ^ 1] if k ^ 1 < len(free) else free[k] for k in range(len(free))]
        for i, j in [(i, targets[i]) for i in used] + list(zip(idle, free)):
            pairs.append((core * count + i, core * count + j))
    return lax.ppermute(x, ("ty", "tx"), pairs)


def exists(step):
    column = lax.axis_index("tx") + step
    return (column >= 0) & (column < lax.axis_size("tx"))


def partner(offsets):
    core = lax.axis_index("ty")
    picked = []
    for steps in offsets:
        place = lax.axis_index("tx") & (len(steps) - 1)
        step = jnp.int32(steps[-1])
        for i in range(len(steps) - 1):
            step = jnp.where(place == i, steps[i], step)
        picked.append(step)
    return jnp.where(core == 0, picked[0], picked[1]), jnp.where(core == 0, picked[1], picked[0])


def pack_kernel(
    counts, footprints, traces, order, centres, movie,
    packed, ordering, film, patch_buf, trace_buf, order_buf, centre_buf, numbers, sems,
):
    pairs = (
        (order, order_buf),
        (centres, centre_buf),
        (footprints, patch_buf),
        (traces, trace_buf),
        (movie, film),
    )
    copies = [pltpu.make_async_copy(a, b, sems.at[i]) for i, (a, b) in enumerate(pairs)]
    for copy in copies:
        copy.start()
    slots, width = patch_buf.shape
    numbers[...] = jnp.zeros_like(numbers)
    for copy in copies[:4]:
        copy.wait()
    numbers[0:1, 0:slots] = order_buf[...].astype(jnp.float32)
    numbers[1:3, 0:slots] = centre_buf[...].astype(jnp.float32)
    numbers[3:4, :] = jnp.full((1, LANES), counts[0, 0], jnp.int32).astype(jnp.float32)
    ordering[...] = order_buf[...]
    packed[:, :width] = patch_buf[...]
    packed[:, width:width + LANES] = trace_buf[...]
    packed[:, width + LANES:] = numbers[...].astype(jnp.bfloat16)
    copies[4].wait()


def paint_tiles(
    sources, rows, columns, canvas, start, patches, numbers, table, sem, prepare=None
):
    slots = sources[0].shape[0]
    total = start.shape[0]
    block = slots // BLOCKS
    group = 2 * block
    source = 3 * group
    pixels = PATCH * PATCH // LANES
    width = pixels * LANES

    heads = [ref[0:16, width + LANES:].astype(jnp.float32) for ref in sources]
    spare = [jnp.zeros((8 - len(sources), LANES), jnp.float32)]
    ordering, top, left, count = (
        jnp.concatenate([head[i:i + 1, :] for head in heads] + spare, axis=0).astype(jnp.int32)
        for i in range(4)
    )
    row = lax.broadcasted_iota(jnp.int32, (8, LANES), 0)
    tile_row = jnp.zeros((8, LANES), jnp.int32)
    tile_col = jnp.zeros((8, LANES), jnp.int32)
    for t in range(len(sources)):
        tile_row = jnp.where(row == t, rows[t], tile_row)
        tile_col = jnp.where(row == t, columns[t], tile_col)
        count = jnp.where((row == t) & jnp.logical_not(exists(columns[t])), 0, count)
    slot_of = lax.broadcasted_iota(jnp.int32, (8, LANES), 1)
    live = (ordering < count[:, 0:1]).astype(jnp.int32)
    top = take_lanes(top, ordering) + tile_row * PATCH
    left = take_lanes(left, ordering) + tile_col * PATCH
    odd = top & 1
    spot = (
        lax.div(slot_of, block) * source
        + (tile_col + 1) * group
        + tile_row * block
        + lax.rem(slot_of, block)
        + lax.shift_right_logical(top, 1) * total
    )
    shift = left + 32 * odd
    fields = [(row * slots + ordering) * pixels, spot, left, left + PATCH * live, odd]
    fields += [(shift + 32 * m) & (LANES - 1) for m in range(4)]
    for i, field in enumerate(fields):
        numbers[i * 8:(i + 1) * 8, :] = field
    fetch = pltpu.make_async_copy(numbers, table, sem)
    fetch.start()

    if prepare is not None:
        prepare()
    for t, ref in enumerate(sources):
        for k in range(pixels):
            patches[pl.ds(t * slots * pixels + k, slots, stride=pixels), :] = ref[
                :, k * LANES:(k + 1) * LANES
            ].astype(jnp.float32)
        which = lax.broadcasted_iota(jnp.int32, (slots, slots), 0)
        chosen = (which == ordering[t:t + 1, :slots]) & (which < count[t:t + 1, 0:1])
        trail = lax.dot_general(
            chosen.astype(jnp.bfloat16),
            ref[:, width:width + LANES],
            (((0,), (0,)), ((), ())),
            preferred_element_type=jnp.float32,
        )
        for q in range(BLOCKS):
            at = q * source + (columns[t] + 1) * group + rows[t] * block
            start[pl.ds(pl.multiple_of(at, block), block), :] = trail[q * block:(q + 1) * block]
    fetch.wait()

    lane = lax.broadcasted_iota(jnp.int32, (pixels, LANES), 1)
    sub = lax.broadcasted_iota(jnp.int32, (pixels, LANES), 0)
    low = lane < LANES // 2
    low_first = low & (sub == 0)
    inner = lane & (LANES // 2 - 1)

    for t in range(len(sources)):
        for s in range(slots):
            origin, at, begins, ends, odd_row, *turns = (
                table[i * 8 + t, s] for i in range(len(fields))
            )
            value = patches[pl.ds(pl.multiple_of(origin, pixels), pixels), :]
            turned = [pltpu.roll(value, turn, 1) for turn in turns]
            down = pltpu.roll(turned[0], 1, 0)
            is_odd = jnp.broadcast_to(odd_row, sub.shape) > 0
            inside = (inner >= begins) & (inner < ends)
            first = jnp.where(is_odd, jnp.where(sub == 0, 0.0, down), turned[0])
            even_rows = jnp.where(inside, jnp.where(low, first, turned[1]), 0.0)
            odd_rows = jnp.where(inside, jnp.where(low, turned[2], turned[3]), 0.0)
            last = jnp.where(inside & low_first & is_odd, down, 0.0)
            canvas[pl.ds(at, pixels, stride=2 * total), :] = even_rows
            canvas[pl.ds(at + total, pixels, stride=2 * total), :] = odd_rows
            canvas[pl.ds(at + 2 * pixels * total, 1), :] = last[0:1, :]


def own_kernel(own, pair, canvas, start, patches, numbers, table, sem):
    core = lax.axis_index("ty")

    def clear():
        canvas[...] = jnp.zeros_like(canvas)

    paint_tiles(
        (own, pair), (core, 1 - core), (0, 0),
        canvas, start, patches, numbers, table, sem, clear,
    )


def near_kernel(
    canvas_own, start_own, first, second, first_other, second_other,
    canvas, start, mine, links, scale, begin, coupling, begin_near,
    patches, numbers, table, sem,
):
    slots = first.shape[0]
    total = start.shape[0]
    group = 2 * slots // BLOCKS
    source = 3 * group
    depth = canvas.shape[0] // total
    core = lax.axis_index("ty")
    step = 2 * core - 1
    paint_tiles(
        (first, second, first_other, second_other),
        (core, core, 1 - core, 1 - core),
        (step, -step, -step, step),
        canvas, start, patches, numbers, table, sem,
    )

    margins = jnp.zeros((2 * slots, total), jnp.float32)
    edge = PATCH // 8
    for step in range(depth // 2):
        at = 2 * step * total
        painted = jnp.concatenate(
            [canvas[at:at + total, :], canvas[at + total:at + 2 * total, :]], axis=1
        ).astype(jnp.bfloat16)
        targets = jnp.concatenate(
            [painted[q * source + group:q * source + 2 * group] for q in range(BLOCKS)], axis=0
        )
        margins += lax.dot_general(
            targets, painted, (((1,), (1,)), ((), ())), preferred_element_type=jnp.float32
        )
        if edge <= step < depth // 2 - edge:
            mine[step - edge] = targets

    coupling[...] = jnp.dot(
        margins, start[...], precision=precise, preferred_element_type=jnp.float32
    )
    line = lax.broadcasted_iota(jnp.int32, margins.shape, 0)
    column = lax.broadcasted_iota(jnp.int32, margins.shape, 1)
    matching = column == (line // group) * source + group + line % group
    diagonal = jnp.sum(jnp.where(matching, margins, 0.0), axis=1, keepdims=True)
    diagonal = jnp.where(diagonal > 0.0, diagonal, 1.0)
    scale[...] = jnp.broadcast_to(diagonal, scale.shape)
    for q in range(BLOCKS):
        begin[q * group:(q + 1) * group, :] = start[q * source + group:q * source + 2 * group, :]
    for i, q in enumerate((1, 2)):
        for side in range(2):
            at = q * source + 2 * side * group
            row = (2 * i + side) * group
            begin_near[row:row + group, :] = start[at:at + group, :]
    share = margins / diagonal
    for i, q in enumerate((1, 2, 3)):
        links[i * group:(i + 1) * group, :] = share[q * group:(q + 1) * group, :LANES]
    links[3 * group:4 * group, :total - LANES] = share[3 * group:4 * group, LANES:]


def drive_kernel(
    mine, links, scale, begin, coupling, film_own, film_pair, film_direct, film_other,
    near, across, cross, level, film,
):
    core = lax.axis_index("ty")
    side_direct = 2 * core - 1
    side_other = -side_direct
    height = film_own.shape[0]
    half = PATCH // 2
    group = links.shape[0] // 4

    def row_of(a):
        return pl.ds(pl.multiple_of(a * height, height), height)

    film[row_of(core), half:half + PATCH, :] = film_own[...]
    film[row_of(1 - core), half:half + PATCH, :] = film_pair[...]
    for ref, side, nearest in ((film_direct, side_direct, core), (film_other, side_other, 1 - core)):
        for u in range(2):
            row = row_of(nearest if u == 0 else 1 - nearest)
            part = ref[u * height:(u + 1) * height]
            part = jnp.where(exists(side), part, jnp.zeros_like(part))

            @pl.when(side < 0)
            def _():
                film[row, 0:half, :] = part

            @pl.when(side >= 0)
            def _():
                film[row, half + PATCH:2 * PATCH, :] = part

    drive = jnp.zeros(coupling.shape, jnp.float32)
    for step in range(mine.shape[0]):
        pixels_here = film[step * 4:(step + 1) * 4].reshape(mine.shape[2], -1)
        drive += jnp.dot(mine[step], pixels_here, preferred_element_type=jnp.float32)
    level[...] = begin[...] + (drive - coupling[...]) / scale[...]

    def rows_of(x, q):
        return x[q * group:(q + 1) * group, :]

    change = jnp.maximum(rows_of(level, 0), 0.0) - rows_of(begin, 0)
    varied = jnp.where(core == 0, rows_of(level, 2), rows_of(begin, 1))
    common = (change, rows_of(level, 1), rows_of(links, 0))
    for ref, rest in (
        (near, (varied, rows_of(links, 1))),
        (across, (rows_of(level, 2), rows_of(links, 1))),
        (cross, (rows_of(begin, 1),)),
    ):
        for i, piece in enumerate(common + rest):
            ref[i * group:(i + 1) * group, :] = piece


def sweep_kernel(
    level, begin, links, begin_near, near_direct, near_other, across_direct, across_other,
    cross_direct, cross_other, order, out, box, current,
):
    slots = out.shape[0]
    block = slots // BLOCKS
    group = 2 * block
    reach = BLOCKS - 1
    refs = (near_direct, near_other, across_direct, across_other, cross_direct, cross_other)
    steps = (*partner(EDGES), *partner(ACROSS), *partner(CROSS))
    for ref, step in zip(refs, steps):
        box[reach + step, 0:ref.shape[0], :] = jnp.where(exists(step), ref[...], 0.0)

    def halves(x):
        high = x.astype(jnp.bfloat16)
        return high, (x - high.astype(jnp.float32)).astype(jnp.bfloat16)

    def product(a, b):
        (a1, a2), (b1, b2) = halves(a), halves(b)
        return sum(
            jnp.dot(x, y, preferred_element_type=jnp.float32)
            for x, y in ((a1, b1), (a1, b2), (a2, b1))
        )

    def block_of(x, i):
        return x[i * group:(i + 1) * group, :]

    def part(j, i):
        return box[j, i * group:(i + 1) * group, :]

    lane = lax.broadcasted_iota(jnp.int32, (group, LANES), 1)
    near = 3 * group

    def band(share, begins, target):
        kept = jnp.where((lane >= begins) & (lane < begins + near), share, 0.0)
        return pltpu.roll(kept, (target - begins) % LANES, 1)

    width = 2 * reach + 1
    spare = jnp.zeros((LANES - width * group, LANES), jnp.float32)
    first = jnp.maximum(block_of(level, 0), 0.0)
    change0 = [
        first - block_of(begin, 0) if j == reach else part(j, 0) for j in range(width)
    ]
    change0 = jnp.concatenate(change0 + [spare], axis=0)

    inner = range(1, width - 1)
    levels = [block_of(level, 1) if j == reach else part(j, 1) for j in inner]
    shares = [block_of(links, 0) if j == reach else part(j, 2) for j in inner]
    begins = [
        part(1, 3), block_of(begin_near, 0), block_of(begin, 1), block_of(begin_near, 1), part(5, 3)
    ]
    shares = [band(share, 0, (j - 1) * group) for j, share in zip(inner, shares)]
    renewed1 = jnp.maximum(
        jnp.concatenate(levels, axis=0) - product(jnp.concatenate(shares, axis=0), change0), 0.0
    )
    change1 = renewed1 - jnp.concatenate(begins, axis=0)
    spare = jnp.zeros((LANES - change1.shape[0], LANES), jnp.float32)
    changes = jnp.concatenate([change0, change1, spare], axis=0)

    inner = range(2, width - 2)
    levels = [block_of(level, 2) if j == reach else part(j, 3) for j in inner]
    shares = [block_of(links, 1) if j == reach else part(j, 4) for j in inner]
    begins = [block_of(begin_near, 2), block_of(begin, 2), block_of(begin_near, 3)]
    shares = [
        jnp.concatenate(
            [band(share, 0, (j - 1) * group), band(share, near, (j - 2) * group)], axis=1
        )
        for j, share in zip(inner, shares)
    ]
    renewed2 = jnp.maximum(
        jnp.concatenate(levels, axis=0) - product(jnp.concatenate(shares, axis=0), changes), 0.0
    )
    change2 = renewed2 - jnp.concatenate(begins, axis=0)

    middle = (reach - 1) * group
    changes = jnp.concatenate(
        [change0[middle:middle + near], change1[middle - group:middle - group + near], change2],
        axis=0,
    )
    share = jnp.concatenate([block_of(links, 2), block_of(links, 3)], axis=1)
    share = share[:, :3 * near]
    current[0:group, :] = first
    current[group:2 * group, :] = renewed1[middle:middle + group]
    current[2 * group:3 * group, :] = renewed2[group:2 * group]
    current[3 * group:4 * group, :] = jnp.maximum(
        block_of(level, 3) - product(share, changes), 0.0
    )
    row = pl.multiple_of(lax.axis_index("ty") * block, block)
    ordered = jnp.concatenate(
        [current[pl.ds(q * group + row, block), :] for q in range(BLOCKS)], axis=0
    )
    place = lax.broadcasted_iota(jnp.int32, (slots, slots), 0) == order[...]
    out[...] = jnp.dot(
        place.astype(jnp.float32), ordered, precision=precise, preferred_element_type=jnp.float32
    )


def call(kernel, outs, scratch, megabytes, spaces=None, cost=None, aliases={}):
    def run(*operands):
        return pl.pallas_call(
            kernel,
            out_shape=[jax.ShapeDtypeStruct(*out) for out in outs],
            in_specs=[
                pl.BlockSpec(memory_space=space)
                for space in spaces or [pltpu.VMEM] * len(operands)
            ],
            out_specs=[pl.BlockSpec(memory_space=pltpu.VMEM)] * len(outs),
            scratch_shapes=scratch,
            compiler_params=pltpu.CompilerParams(vmem_limit_bytes=megabytes << 20),
            cost_estimate=cost,
            input_output_aliases=aliases,
        )(*operands)

    return run


def strip_body(movie, footprints, centres, traces, counts, order):
    height, _, frames = movie.shape
    slots = footprints.shape[2]
    area = footprints.shape[3]
    half = PATCH // 2
    group = 2 * slots // BLOCKS
    total = 6 * slots
    bf16, f32 = jnp.bfloat16, jnp.float32

    given = (footprints[0, 0], traces[0, 0], order[0], centres[0, 0].T, movie)
    packed, ordering, film = call(
        pack_kernel,
        [((slots, area + 2 * LANES), bf16), ((1, slots), jnp.int32), (movie.shape, bf16)],
        [
            pltpu.VMEM((slots, area), bf16),
            pltpu.VMEM((slots, frames), bf16),
            pltpu.VMEM((1, slots), jnp.int32),
            pltpu.VMEM((2, slots), jnp.int32),
            pltpu.VMEM((slots, LANES), f32),
            pltpu.SemaphoreType.DMA((len(given),)),
        ],
        4,
        [pltpu.SMEM] + [pltpu.HBM] * len(given),
    )(counts, *(pltpu.with_memory_space_constraint(x, pltpu.HBM) for x in given))
    pair_film = swap(movie)
    first = beside(packed)
    second = beside(packed, -1)
    pair = swap(packed)
    edge = jnp.where(lax.axis_index("ty") == 0, half, 0)
    edges = jnp.concatenate(
        [lax.dynamic_slice_in_dim(x, edge, half, axis=1) for x in (film, pair_film)], axis=0
    )
    film_direct = beside(edges)
    first_other = swap(first)
    second_other = swap(second)
    film_other = swap(film_direct)

    canvas = ((2 * height + PATCH) // 2 * total, LANES)

    def painting(tiles):
        return [
            pltpu.VMEM((tiles * slots * area // LANES, LANES), f32),
            pltpu.VMEM((72, LANES), jnp.int32),
            pltpu.SMEM((72, LANES), jnp.int32),
            pltpu.SemaphoreType.DMA,
        ]

    own_canvas, own_start = call(
        own_kernel,
        [(canvas, f32), ((total, frames), f32)],
        painting(2),
        4,
        cost=pl.CostEstimate(flops=1_500_000_000, bytes_accessed=0, transcendentals=0),
    )(packed, pair)
    *_, mine, links, scale, begin, coupling, begin_near = call(
        near_kernel,
        [
            (canvas, f32),
            ((total, frames), f32),
            ((height // 2, 2 * slots, 2 * LANES), bf16),
            ((4 * group, LANES), f32),
            ((2 * slots, frames), f32),
            ((2 * slots, frames), f32),
            ((2 * slots, frames), f32),
            ((4 * group, frames), f32),
        ],
        painting(4),
        8,
        cost=pl.CostEstimate(flops=3_000_000_000, bytes_accessed=0, transcendentals=0),
        aliases={0: 0, 1: 1},
    )(own_canvas, own_start, first, second, first_other, second_other)
    near, across, cross, level = call(
        drive_kernel,
        [((rows * group, frames), f32) for rows in (5, 5, 4, 4)],
        [pltpu.VMEM((2 * height, 2 * PATCH, frames), bf16)],
        8,
    )(mine, links, scale, begin, coupling, film, pair_film, film_direct, film_other)

    across_direct = pairwise(across, ACROSS)
    cross_direct = pairwise(cross, CROSS)
    near_direct = pairwise(near, EDGES)
    across_other = swap(across_direct)
    cross_other = swap(cross_direct)
    near_other = swap(near_direct)
    (result,) = call(
        sweep_kernel,
        [((slots, frames), f32)],
        [
            pltpu.VMEM((2 * BLOCKS - 1, 5 * group, frames), f32),
            pltpu.VMEM((4 * group, frames), f32),
        ],
        4,
    )(
        level, begin, links, begin_near, near_direct, near_other, across_direct, across_other,
        cross_direct, cross_other, ordering,
    )
    return result[None, None]


def body(movie, footprints, centres, traces, counts, order):
    strip = (
        lax.axis_size("ty") == 2
        and movie.shape == (PATCH, PATCH, LANES)
        and footprints.shape[2] == PATCH
    )
    chosen = strip_body if strip else general_body
    return chosen(movie, footprints, centres, traces, counts, order)


def solution(mesh):
    in_specs = (
        P("ty", "tx", None),
        P("ty", "tx", None, None),
        P("ty", "tx", None, None),
        P("ty", "tx", None, None),
        P("ty", "tx"),
        P("ty", "tx", None),
    )
    out_specs = P("ty", "tx", None, None)
    return jax.shard_map(body, mesh=mesh, in_specs=in_specs, out_specs=out_specs, check_vma=False)
```

```python
import jax
import jax.numpy as jnp
from jax import lax
from jax.experimental import pallas as pl
from jax.experimental.pallas import tpu as pltpu
from jax.sharding import PartitionSpec as P

BLOCKS = 4
PATCH = 32
LANES = 128


precise = lax.Precision.HIGHEST


def extended(x, sides, width):
    for axis, dim in sides:
        devices, length = (lax.axis_size(axis), x.shape[dim])
        up = [(i, (i + 1) % devices) for i in range(devices - 1)]
        down = [(j, i) for i, j in up]
        last = lax.slice_in_dim(x, length - width, length, axis=dim)
        first = lax.slice_in_dim(x, 0, width, axis=dim)
        before = lax.ppermute(last, axis, up)
        after = lax.ppermute(first, axis, down)
        x = jnp.concatenate([before, x, after], axis=dim)
    return x


def placement(anchors, extent, length):
    across = jnp.arange(extent, dtype=jnp.int32)[None, :, None]
    inside = jnp.arange(length, dtype=jnp.int32)[None, None, :]
    return (across == anchors[:, None, None] + inside).astype(jnp.bfloat16)


def paint(patches, top_rows, left_cols, canvas_rows, canvas_cols):
    rows_hot = placement(top_rows, canvas_rows, PATCH)
    cols_hot = placement(left_cols, canvas_cols, PATCH)
    spread = jnp.einsum(
        "kyi,kij->kyj", rows_hot, patches, preferred_element_type=jnp.float32
    ).astype(jnp.bfloat16)
    canvas = jnp.einsum(
        "kyj,kxj->kyx", spread, cols_hot, preferred_element_type=jnp.float32
    ).astype(jnp.bfloat16)
    return canvas.reshape(patches.shape[0], canvas_rows * canvas_cols)


def general_body(movie, footprints, centres, traces, counts, order):
    tile_side = movie.shape[0]
    frame_count = movie.shape[2]
    slot_count = footprints.shape[2]
    half_patch = PATCH // 2
    block_rows = slot_count // BLOCKS
    ordering = order[0, 0]
    alive_mask = ordering < counts[0, 0]
    selector = ordering[:, None] == jnp.arange(slot_count, dtype=jnp.int32)[None, :]
    chooser = (selector & alive_mask[:, None]).astype(jnp.bfloat16)
    own_flat = jnp.dot(chooser, footprints[0, 0], preferred_element_type=jnp.float32).astype(
        jnp.bfloat16
    )
    first_traces = jnp.dot(chooser, traces[0, 0], preferred_element_type=jnp.float32).astype(
        jnp.bfloat16
    )
    picker = selector.astype(jnp.int32)
    own_pos = jnp.sum(picker[:, :, None] * centres[0, 0][None, :, :], axis=1)
    near_flat, near_pos, near_traces = (
        extended(own_flat[None, None], (("ty", 0), ("tx", 1)), 1),
        extended(own_pos.astype(jnp.bfloat16)[None, None], (("ty", 0), ("tx", 1)), 1),
        extended(first_traces[None, None], (("ty", 0), ("tx", 1)), 1),
    )
    offsets = (jnp.arange(3, dtype=jnp.int32) - 1) * tile_side
    near_rows = (near_pos[..., 0].astype(jnp.int32) + offsets[:, None, None]).reshape(
        9 * slot_count
    )
    near_cols = (near_pos[..., 1].astype(jnp.int32) + offsets[None, :, None]).reshape(
        9 * slot_count
    )
    own_rows = own_pos[:, 0]
    own_cols = own_pos[:, 1]
    own_patch = own_flat.reshape(slot_count, PATCH, PATCH)
    near_patch = near_flat.reshape(9 * slot_count, PATCH, PATCH)
    canvas_side = tile_side + 2 * half_patch
    own_canvas = paint(own_patch, own_rows, own_cols, canvas_side, canvas_side)
    near_canvas = paint(near_patch, near_rows, near_cols, canvas_side, canvas_side)
    margins = lax.dot_general(
        own_canvas, near_canvas, (((1,), (1,)), ((), ())), preferred_element_type=jnp.float32
    )
    by_source = margins.reshape(slot_count, 9, slot_count)
    padded_movie = extended(movie, (("ty", 0), ("tx", 1)), half_patch)
    drive_term = jnp.dot(
        own_canvas,
        padded_movie.reshape(canvas_side * canvas_side, frame_count),
        preferred_element_type=jnp.float32,
    )
    current = first_traces.astype(jnp.float32)
    coupling = jnp.dot(
        margins,
        near_traces.reshape(9 * slot_count, frame_count).astype(jnp.float32),
        precision=precise,
        preferred_element_type=jnp.float32,
    )
    diagonal = jnp.diagonal(by_source[:, 4])
    denominator = jnp.where(alive_mask, diagonal, 1.0)
    for block_index in range(BLOCKS):
        lower = block_index * block_rows
        upper = lower + block_rows
        previous = current[lower:upper]
        renewed = jnp.maximum(
            previous
            + (drive_term[lower:upper] - coupling[lower:upper]) / denominator[lower:upper, None],
            0.0,
        )
        renewed = jnp.where(alive_mask[lower:upper, None], renewed, 0.0)
        current = current.at[lower:upper].set(renewed)
        if block_index + 1 < BLOCKS:
            change = extended((renewed - previous)[None, None], (("ty", 0), ("tx", 1)), 1)
            columns = by_source[:, :, lower:upper].reshape(slot_count, 9 * block_rows)
            coupling = coupling + jnp.dot(
                columns,
                change.reshape(9 * block_rows, frame_count),
                precision=precise,
                preferred_element_type=jnp.float32,
            )
    result = lax.dot_general(
        selector.astype(jnp.float32),
        current,
        (((0,), (0,)), ((), ())),
        precision=precise,
        preferred_element_type=jnp.float32,
    )
    return result[None, None]


EDGES = ((1, -1, 1, -1), (2, 2, -2, -2))
ACROSS = ((-1, -3, 3, 1), (3, 1, -1, -3))
CROSS = ((-2, -2, 2, 2), (-3, 3, -3, 3))


def take_lanes(values, lanes):
    return jnp.take_along_axis(values, lanes, axis=1, mode="promise_in_bounds")


def thirds(x):
    parts = []
    for _ in range(3):
        parts.append(x.astype(jnp.bfloat16))
        x = x - parts[-1].astype(jnp.float32)
    return parts


def swap(x):
    return lax.ppermute(x, "ty", [(0, 1), (1, 0)])


def beside(x, turn=1):
    count = lax.axis_size("tx")
    ring = list(range(count)) + list(range(2 * count - 1, count - 1, -1))
    ring = ring[::turn]
    return lax.ppermute(x, ("ty", "tx"), list(zip(ring, ring[1:] + ring[:1])))


def pairwise(x, offsets):
    count = lax.axis_size("tx")
    pairs = []
    for core, steps in enumerate(offsets):
        targets = [i + steps[i % len(steps)] for i in range(count)]
        used = [i for i in range(count) if 0 <= targets[i] < count]
        free = sorted(set(range(count)) - {targets[i] for i in used})
        idle = [i for i in range(count) if i not in used]
        if any(i == j for i, j in zip(idle, free)):
            free = [free[k ^ 1] if k ^ 1 < len(free) else free[k] for k in range(len(free))]
        for i, j in [(i, targets[i]) for i in used] + list(zip(idle, free)):
            pairs.append((core * count + i, core * count + j))
    return lax.ppermute(x, ("ty", "tx"), pairs)


def exists(step):
    column = lax.axis_index("tx") + step
    return (column >= 0) & (column < lax.axis_size("tx"))


def partner(offsets):
    core = lax.axis_index("ty")
    picked = []
    for steps in offsets:
        place = lax.axis_index("tx") & (len(steps) - 1)
        step = jnp.int32(steps[-1])
        for i in range(len(steps) - 1):
            step = jnp.where(place == i, steps[i], step)
        picked.append(step)
    return jnp.where(core == 0, picked[0], picked[1]), jnp.where(core == 0, picked[1], picked[0])


def pack_kernel(
    counts, footprints, traces, order, centres, movie,
    packed, ordering, film, patch_buf, trace_buf, order_buf, centre_buf, numbers, sems,
):
    pairs = (
        (order, order_buf),
        (centres, centre_buf),
        (footprints, patch_buf),
        (traces, trace_buf),
        (movie, film),
    )
    copies = [pltpu.make_async_copy(a, b, sems.at[i]) for i, (a, b) in enumerate(pairs)]
    for copy in copies:
        copy.start()
    slots, width = patch_buf.shape
    numbers[...] = jnp.zeros_like(numbers)
    for copy in copies[:4]:
        copy.wait()
    numbers[0:1, 0:slots] = order_buf[...].astype(jnp.float32)
    numbers[1:3, 0:slots] = centre_buf[...].astype(jnp.float32)
    numbers[3:4, :] = jnp.full((1, LANES), counts[0, 0], jnp.int32).astype(jnp.float32)
    ordering[...] = order_buf[...]
    packed[:, :width] = patch_buf[...]
    packed[:, width:width + LANES] = trace_buf[...]
    packed[:, width + LANES:] = numbers[...].astype(jnp.bfloat16)
    copies[4].wait()


def paint_tiles(
    sources, rows, columns, canvas, start, patches, numbers, table, sem, prepare=None
):
    slots = sources[0].shape[0]
    total = start.shape[0]
    block = slots // BLOCKS
    group = 2 * block
    source = 3 * group
    pixels = PATCH * PATCH // LANES
    width = pixels * LANES

    heads = [ref[0:16, width + LANES:].astype(jnp.float32) for ref in sources]
    spare = [jnp.zeros((8 - len(sources), LANES), jnp.float32)]
    ordering, top, left, count = (
        jnp.concatenate([head[i:i + 1, :] for head in heads] + spare, axis=0).astype(jnp.int32)
        for i in range(4)
    )
    row = lax.broadcasted_iota(jnp.int32, (8, LANES), 0)
    tile_row = jnp.zeros((8, LANES), jnp.int32)
    tile_col = jnp.zeros((8, LANES), jnp.int32)
    for t in range(len(sources)):
        tile_row = jnp.where(row == t, rows[t], tile_row)
        tile_col = jnp.where(row == t, columns[t], tile_col)
        count = jnp.where((row == t) & jnp.logical_not(exists(columns[t])), 0, count)
    slot_of = lax.broadcasted_iota(jnp.int32, (8, LANES), 1)
    live = (ordering < count[:, 0:1]).astype(jnp.int32)
    top = take_lanes(top, ordering) + tile_row * PATCH
    left = take_lanes(left, ordering) + tile_col * PATCH
    odd = top & 1
    spot = (
        lax.div(slot_of, block) * source
        + (tile_col + 1) * group
        + tile_row * block
        + lax.rem(slot_of, block)
        + lax.shift_right_logical(top, 1) * total
    )
    shift = left + 32 * odd
    fields = [(row * slots + ordering) * pixels, spot, left, left + PATCH * live, odd]
    fields += [(shift + 32 * m) & (LANES - 1) for m in range(4)]
    for i, field in enumerate(fields):
        numbers[i * 8:(i + 1) * 8, :] = field
    fetch = pltpu.make_async_copy(numbers, table, sem)
    fetch.start()

    if prepare is not None:
        prepare()
    for t, ref in enumerate(sources):
        for k in range(pixels):
            patches[pl.ds(t * slots * pixels + k, slots, stride=pixels), :] = ref[
                :, k * LANES:(k + 1) * LANES
            ].astype(jnp.float32)
        which = lax.broadcasted_iota(jnp.int32, (slots, slots), 0)
        chosen = (which == ordering[t:t + 1, :slots]) & (which < count[t:t + 1, 0:1])
        trail = lax.dot_general(
            chosen.astype(jnp.bfloat16),
            ref[:, width:width + LANES],
            (((0,), (0,)), ((), ())),
            preferred_element_type=jnp.float32,
        )
        for q in range(BLOCKS):
            at = q * source + (columns[t] + 1) * group + rows[t] * block
            start[pl.ds(pl.multiple_of(at, block), block), :] = trail[q * block:(q + 1) * block]
    fetch.wait()

    lane = lax.broadcasted_iota(jnp.int32, (pixels, LANES), 1)
    sub = lax.broadcasted_iota(jnp.int32, (pixels, LANES), 0)
    low = lane < LANES // 2
    low_first = low & (sub == 0)
    inner = lane & (LANES // 2 - 1)

    for t in range(len(sources)):
        for s in range(slots):
            origin, at, begins, ends, odd_row, *turns = (
                table[i * 8 + t, s] for i in range(len(fields))
            )
            value = patches[pl.ds(pl.multiple_of(origin, pixels), pixels), :]
            turned = [pltpu.roll(value, turn, 1) for turn in turns]
            down = pltpu.roll(turned[0], 1, 0)
            is_odd = jnp.broadcast_to(odd_row, sub.shape) > 0
            inside = (inner >= begins) & (inner < ends)
            first = jnp.where(is_odd, jnp.where(sub == 0, 0.0, down), turned[0])
            even_rows = jnp.where(inside, jnp.where(low, first, turned[1]), 0.0)
            odd_rows = jnp.where(inside, jnp.where(low, turned[2], turned[3]), 0.0)
            last = jnp.where(inside & low_first & is_odd, down, 0.0)
            canvas[pl.ds(at, pixels, stride=2 * total), :] = even_rows
            canvas[pl.ds(at + total, pixels, stride=2 * total), :] = odd_rows
            canvas[pl.ds(at + 2 * pixels * total, 1), :] = last[0:1, :]


def own_kernel(own, pair, canvas, start, patches, numbers, table, sem):
    core = lax.axis_index("ty")

    def clear():
        canvas[...] = jnp.zeros_like(canvas)

    paint_tiles(
        (own, pair), (core, 1 - core), (0, 0),
        canvas, start, patches, numbers, table, sem, clear,
    )


def near_kernel(
    canvas_own, start_own, first, second, first_other, second_other,
    canvas, start, patches, numbers, table, sem,
):
    core = lax.axis_index("ty")
    step = 2 * core - 1
    paint_tiles(
        (first, second, first_other, second_other),
        (core, core, 1 - core, 1 - core),
        (step, -step, -step, step),
        canvas, start, patches, numbers, table, sem,
    )


def margins_kernel(canvas, start, mine, links, scale, begin, coupling, begin_near):
    total = start.shape[0]
    slots = total // 6
    group = 2 * slots // BLOCKS
    source = 3 * group
    depth = canvas.shape[0] // total
    margins = jnp.zeros((2 * slots, total), jnp.float32)
    edge = PATCH // 8
    for step in range(depth // 2):
        at = 2 * step * total
        painted = jnp.concatenate(
            [canvas[at:at + total, :], canvas[at + total:at + 2 * total, :]], axis=1
        ).astype(jnp.bfloat16)
        targets = jnp.concatenate(
            [painted[q * source + group:q * source + 2 * group] for q in range(BLOCKS)], axis=0
        )
        margins += lax.dot_general(
            targets, painted, (((1,), (1,)), ((), ())), preferred_element_type=jnp.float32
        )
        if edge <= step < depth // 2 - edge:
            mine[step - edge] = targets

    begins = start[...].astype(jnp.bfloat16)
    coupling[...] = sum(
        jnp.dot(x, begins, preferred_element_type=jnp.float32) for x in thirds(margins)
    )
    line = lax.broadcasted_iota(jnp.int32, margins.shape, 0)
    column = lax.broadcasted_iota(jnp.int32, margins.shape, 1)
    matching = column == (line // group) * source + group + line % group
    diagonal = jnp.sum(jnp.where(matching, margins, 0.0), axis=1, keepdims=True)
    diagonal = jnp.where(diagonal > 0.0, diagonal, 1.0)
    scale[...] = jnp.broadcast_to(diagonal, scale.shape)
    for q in range(BLOCKS):
        begin[q * group:(q + 1) * group, :] = start[q * source + group:q * source + 2 * group, :]
    for i, q in enumerate((1, 2)):
        for side in range(2):
            at = q * source + 2 * side * group
            row = (2 * i + side) * group
            begin_near[row:row + group, :] = start[at:at + group, :]
    share = margins / diagonal
    for i, q in enumerate((1, 2, 3)):
        links[i * group:(i + 1) * group, :] = share[q * group:(q + 1) * group, :LANES]
    links[3 * group:4 * group, :total - LANES] = share[3 * group:4 * group, LANES:]


def drive_kernel(
    mine, links, scale, begin, coupling, film_own, film_pair, film_direct, film_other,
    near, across, cross, level, film,
):
    core = lax.axis_index("ty")
    side_direct = 2 * core - 1
    side_other = -side_direct
    height = film_own.shape[0]
    half = PATCH // 2
    group = links.shape[0] // 4

    def row_of(a):
        return pl.ds(pl.multiple_of(a * height, height), height)

    film[row_of(core), half:half + PATCH, :] = film_own[...]
    film[row_of(1 - core), half:half + PATCH, :] = film_pair[...]
    for ref, side, nearest in ((film_direct, side_direct, core), (film_other, side_other, 1 - core)):
        for u in range(2):
            row = row_of(nearest if u == 0 else 1 - nearest)
            part = ref[u * height:(u + 1) * height]
            part = jnp.where(exists(side), part, jnp.zeros_like(part))

            @pl.when(side < 0)
            def _():
                film[row, 0:half, :] = part

            @pl.when(side >= 0)
            def _():
                film[row, half + PATCH:2 * PATCH, :] = part

    drive = jnp.zeros(coupling.shape, jnp.float32)
    for step in range(mine.shape[0]):
        pixels_here = film[step * 4:(step + 1) * 4].reshape(mine.shape[2], -1)
        drive += jnp.dot(mine[step], pixels_here, preferred_element_type=jnp.float32)
    level[...] = begin[...] + (drive - coupling[...]) / scale[...]

    def rows_of(x, q):
        return x[q * group:(q + 1) * group, :]

    change = jnp.maximum(rows_of(level, 0), 0.0) - rows_of(begin, 0)
    varied = jnp.where(core == 0, rows_of(level, 2), rows_of(begin, 1))
    common = (change, rows_of(level, 1), rows_of(links, 0))
    for ref, rest in (
        (near, (varied, rows_of(links, 1))),
        (across, (rows_of(level, 2), rows_of(links, 1))),
        (cross, (rows_of(begin, 1),)),
    ):
        for i, piece in enumerate(common + rest):
            ref[i * group:(i + 1) * group, :] = piece


def sweep_kernel(
    level, begin, links, begin_near, near_direct, near_other, across_direct, across_other,
    cross_direct, cross_other, order, out, box, current,
):
    slots = out.shape[0]
    block = slots // BLOCKS
    group = 2 * block
    reach = BLOCKS - 1
    refs = (near_direct, near_other, across_direct, across_other, cross_direct, cross_other)
    steps = (*partner(EDGES), *partner(ACROSS), *partner(CROSS))
    for ref, step in zip(refs, steps):
        box[reach + step, 0:ref.shape[0], :] = jnp.where(exists(step), ref[...], 0.0)

    def halves(x):
        high = x.astype(jnp.bfloat16)
        return high, (x - high.astype(jnp.float32)).astype(jnp.bfloat16)

    def product(a, b):
        (a1, a2), (b1, b2) = halves(a), halves(b)
        return sum(
            jnp.dot(x, y, preferred_element_type=jnp.float32)
            for x, y in ((a1, b1), (a1, b2), (a2, b1))
        )

    def block_of(x, i):
        return x[i * group:(i + 1) * group, :]

    def part(j, i):
        return box[j, i * group:(i + 1) * group, :]

    lane = lax.broadcasted_iota(jnp.int32, (group, LANES), 1)
    near = 3 * group

    def band(share, begins, target):
        kept = jnp.where((lane >= begins) & (lane < begins + near), share, 0.0)
        return pltpu.roll(kept, (target - begins) % LANES, 1)

    width = 2 * reach + 1
    spare = jnp.zeros((LANES - width * group, LANES), jnp.float32)
    first = jnp.maximum(block_of(level, 0), 0.0)
    change0 = [
        first - block_of(begin, 0) if j == reach else part(j, 0) for j in range(width)
    ]
    change0 = jnp.concatenate(change0 + [spare], axis=0)

    inner = range(1, width - 1)
    levels = [block_of(level, 1) if j == reach else part(j, 1) for j in inner]
    shares = [block_of(links, 0) if j == reach else part(j, 2) for j in inner]
    begins = [
        part(1, 3), block_of(begin_near, 0), block_of(begin, 1), block_of(begin_near, 1), part(5, 3)
    ]
    shares = [band(share, 0, (j - 1) * group) for j, share in zip(inner, shares)]
    renewed1 = jnp.maximum(
        jnp.concatenate(levels, axis=0) - product(jnp.concatenate(shares, axis=0), change0), 0.0
    )
    change1 = renewed1 - jnp.concatenate(begins, axis=0)
    spare = jnp.zeros((LANES - change1.shape[0], LANES), jnp.float32)
    changes = jnp.concatenate([change0, change1, spare], axis=0)

    inner = range(2, width - 2)
    levels = [block_of(level, 2) if j == reach else part(j, 3) for j in inner]
    shares = [block_of(links, 1) if j == reach else part(j, 4) for j in inner]
    begins = [block_of(begin_near, 2), block_of(begin, 2), block_of(begin_near, 3)]
    shares = [
        jnp.concatenate(
            [band(share, 0, (j - 1) * group), band(share, near, (j - 2) * group)], axis=1
        )
        for j, share in zip(inner, shares)
    ]
    renewed2 = jnp.maximum(
        jnp.concatenate(levels, axis=0) - product(jnp.concatenate(shares, axis=0), changes), 0.0
    )
    change2 = renewed2 - jnp.concatenate(begins, axis=0)

    middle = (reach - 1) * group
    changes = jnp.concatenate(
        [change0[middle:middle + near], change1[middle - group:middle - group + near], change2],
        axis=0,
    )
    share = jnp.concatenate([block_of(links, 2), block_of(links, 3)], axis=1)
    share = share[:, :3 * near]
    current[0:group, :] = first
    current[group:2 * group, :] = renewed1[middle:middle + group]
    current[2 * group:3 * group, :] = renewed2[group:2 * group]
    current[3 * group:4 * group, :] = jnp.maximum(
        block_of(level, 3) - product(share, changes), 0.0
    )
    row = pl.multiple_of(lax.axis_index("ty") * block, block)
    ordered = jnp.concatenate(
        [current[pl.ds(q * group + row, block), :] for q in range(BLOCKS)], axis=0
    )
    place = lax.broadcasted_iota(jnp.int32, (slots, slots), 0) == order[...]
    place = place.astype(jnp.bfloat16)
    out[...] = sum(
        jnp.dot(place, x, preferred_element_type=jnp.float32) for x in thirds(ordered)
    )


def call(kernel, outs, scratch, megabytes, spaces=None, cost=None, aliases={}):
    def run(*operands):
        return pl.pallas_call(
            kernel,
            out_shape=[jax.ShapeDtypeStruct(*out) for out in outs],
            in_specs=[
                pl.BlockSpec(memory_space=space)
                for space in spaces or [pltpu.VMEM] * len(operands)
            ],
            out_specs=[pl.BlockSpec(memory_space=pltpu.VMEM)] * len(outs),
            scratch_shapes=scratch,
            compiler_params=pltpu.CompilerParams(vmem_limit_bytes=megabytes << 20),
            cost_estimate=cost,
            input_output_aliases=aliases,
        )(*operands)

    return run


def strip_body(movie, footprints, centres, traces, counts, order):
    height, _, frames = movie.shape
    slots = footprints.shape[2]
    area = footprints.shape[3]
    half = PATCH // 2
    group = 2 * slots // BLOCKS
    total = 6 * slots
    bf16, f32 = jnp.bfloat16, jnp.float32

    given = (footprints[0, 0], traces[0, 0], order[0], centres[0, 0].T, movie)
    packed, ordering, film = call(
        pack_kernel,
        [((slots, area + 2 * LANES), bf16), ((1, slots), jnp.int32), (movie.shape, bf16)],
        [
            pltpu.VMEM((slots, area), bf16),
            pltpu.VMEM((slots, frames), bf16),
            pltpu.VMEM((1, slots), jnp.int32),
            pltpu.VMEM((2, slots), jnp.int32),
            pltpu.VMEM((slots, LANES), f32),
            pltpu.SemaphoreType.DMA((len(given),)),
        ],
        4,
        [pltpu.SMEM] + [pltpu.HBM] * len(given),
    )(counts, *(pltpu.with_memory_space_constraint(x, pltpu.HBM) for x in given))
    pair_film = swap(movie)
    first = beside(packed)
    second = beside(packed, -1)
    pair = swap(packed)
    edge = jnp.where(lax.axis_index("ty") == 0, half, 0)
    edges = jnp.concatenate(
        [lax.dynamic_slice_in_dim(x, edge, half, axis=1) for x in (film, pair_film)], axis=0
    )
    film_direct = beside(edges)
    first_other = swap(first)
    second_other = swap(second)
    film_other = swap(film_direct)

    canvas = ((2 * height + PATCH) // 2 * total, LANES)

    def painting(tiles):
        return [
            pltpu.VMEM((tiles * slots * area // LANES, LANES), f32),
            pltpu.VMEM((72, LANES), jnp.int32),
            pltpu.SMEM((72, LANES), jnp.int32),
            pltpu.SemaphoreType.DMA,
        ]

    own_canvas, own_start = call(
        own_kernel,
        [(canvas, f32), ((total, frames), f32)],
        painting(2),
        4,
        cost=pl.CostEstimate(flops=1_500_000_000, bytes_accessed=0, transcendentals=0),
    )(packed, pair)
    painted, start = call(
        near_kernel,
        [(canvas, f32), ((total, frames), f32)],
        painting(4),
        4,
        cost=pl.CostEstimate(flops=2_000_000_000, bytes_accessed=0, transcendentals=0),
        aliases={0: 0, 1: 1},
    )(own_canvas, own_start, first, second, first_other, second_other)
    mine, links, scale, begin, coupling, begin_near = call(
        margins_kernel,
        [
            ((height // 2, 2 * slots, 2 * LANES), bf16),
            ((4 * group, LANES), f32),
            ((2 * slots, frames), f32),
            ((2 * slots, frames), f32),
            ((2 * slots, frames), f32),
            ((4 * group, frames), f32),
        ],
        [],
        4,
        cost=pl.CostEstimate(flops=1_500_000_000, bytes_accessed=0, transcendentals=0),
    )(painted, start)
    near, across, cross, level = call(
        drive_kernel,
        [((rows * group, frames), f32) for rows in (5, 5, 4, 4)],
        [pltpu.VMEM((2 * height, 2 * PATCH, frames), bf16)],
        8,
    )(mine, links, scale, begin, coupling, film, pair_film, film_direct, film_other)

    across_direct = pairwise(across, ACROSS)
    cross_direct = pairwise(cross, CROSS)
    near_direct = pairwise(near, EDGES)
    across_other = swap(across_direct)
    cross_other = swap(cross_direct)
    near_other = swap(near_direct)
    (result,) = call(
        sweep_kernel,
        [((slots, frames), f32)],
        [
            pltpu.VMEM((2 * BLOCKS - 1, 5 * group, frames), f32),
            pltpu.VMEM((4 * group, frames), f32),
        ],
        4,
    )(
        level, begin, links, begin_near, near_direct, near_other, across_direct, across_other,
        cross_direct, cross_other, ordering,
    )
    return result[None, None]


def body(movie, footprints, centres, traces, counts, order):
    strip = (
        lax.axis_size("ty") == 2
        and movie.shape == (PATCH, PATCH, LANES)
        and footprints.shape[2] == PATCH
    )
    chosen = strip_body if strip else general_body
    return chosen(movie, footprints, centres, traces, counts, order)


def solution(mesh):
    in_specs = (
        P("ty", "tx", None),
        P("ty", "tx", None, None),
        P("ty", "tx", None, None),
        P("ty", "tx", None, None),
        P("ty", "tx"),
        P("ty", "tx", None),
    )
    out_specs = P("ty", "tx", None, None)
    return jax.shard_map(body, mesh=mesh, in_specs=in_specs, out_specs=out_specs, check_vma=False)
```
